128 devices in a mesh: dp: 8 (over y, x_hi), fsdp: 16 (over z, x_lo, core).
Axes of the slice: x: 4 (x_hi: 2, x_lo: 2; x = x_hi * 2 + x_lo), y: 4, z: 4, core: 2. Of those that a mesh axis runs over, the one named last changes fastest.
Arguments:
- tokens: bfloat16 [49152, 8192], P(('dp', 'fsdp')), may hold values from -6 to 6
- frozen_value_weight: bfloat16 [8192, 1024], P('fsdp'), may hold values from -0.0625 to 0.0625
- adapter_down_weight: bfloat16 [32, 8192, 64], P('dp', 'fsdp'), may hold values from -0.0625 to 0.0625
- adapter_up_weight: bfloat16 [32, 64, 1024], P('dp', None, 'fsdp'), may hold values from -0.75 to 0.75
- output_gradient: bfloat16 [49152, 1024], P(('dp', 'fsdp')), may hold values from -6 to 6
- adapter_per_block: int32 [384], P(('dp', 'fsdp')), may hold values from 0 to 31, as said below
- block_live_count: int32 [384], P(('dp', 'fsdp')), may hold values from 1 to 128
Outputs:
- values: bfloat16 [49152, 1024], P(('dp', 'fsdp'))
- input_gradient: bfloat16 [49152, 8192], P(('dp', 'fsdp'))
- grad_down: float32 [32, 8192, 64], P('dp', 'fsdp')
- grad_up: float32 [32, 64, 1024], P('dp', None, 'fsdp')
The draws below stay inside these ranges and needn't reach their ends.
Inputs may be any that keep to these rules, and one draw needn't show every extreme that they name: `adapter_per_block`: within the blocks of one device the adapter numbers never fall.
All inputs are finite; a program needn't handle non-finite values.
Results may differ from the reference program's by a relative error of at most 0.0038.
Values may be sent and summed in bfloat16 or wider, within the bound.
No kernel may reach another device: no remote copies, remote signals or barrier semaphores. Data moves between devices by JAX's collectives and lax.ppermute only.
A program may use at most 192 MiB of HBM per device.

```python
import jax
import jax.numpy as jnp
from jax import lax

MODEL_WIDTH = 8192
VALUE_WIDTH = 1024
ADAPTER_RANK = 64
ADAPTER_COUNT = 32
BLOCK = 128
TOK_DEV = 384
TOKEN_SLOTS = 49152
N_BLOCKS = 384


def draw_adapter_per_block(key, part):
    per_dev = TOK_DEV // BLOCK
    groups = N_BLOCKS // per_dev
    upper_key, number_key, place_key = jax.random.split(jax.random.fold_in(key, 7), 3)
    upper = jax.random.randint(upper_key, (N_BLOCKS,), 1, ADAPTER_COUNT + 1)
    numbers = jax.random.randint(number_key, (N_BLOCKS,), 0, upper)
    ordered = jnp.sort(numbers.reshape(groups, per_dev), axis=1)
    ordered = ordered.at[0, 0].set(0)
    chosen = jax.random.randint(place_key, (), 1, groups)
    ordered = ordered.at[chosen, per_dev - 1].set(ADAPTER_COUNT - 1)
    return ordered.reshape(N_BLOCKS).astype(jnp.int32)


def set_ends(drawn, key, low, top_value):
    place = [jax.random.randint(jax.random.fold_in(key, axis), (), 0, length) for axis, length in enumerate(drawn.shape)]
    main_axis = drawn.shape.index(max(drawn.shape))
    beside = place[:main_axis] + [(place[main_axis] + 1) % drawn.shape[main_axis]] + place[main_axis + 1:]
    return drawn.at[tuple(place)].set(low).at[tuple(beside)].set(top_value)


def steps_of(own_key, shape, shards, low, top_value):
    loudness, own = 1.0, jax.random.fold_in(own_key, 6)
    for position, parts in shards:
        heights = jnp.exp(jax.random.uniform(jax.random.fold_in(own, position), (parts,), jnp.float32, low / len(shards), top_value / len(shards)))
        loudness = loudness * jnp.repeat(heights, shape[position] // parts).reshape([-1 if axis == position else 1 for axis in range(len(shape))])
    return loudness


def centred(rng, shape, spread, limit, shards=(), kind=jnp.bfloat16):
    drawn = jax.random.normal(rng, shape, jnp.float32) * spread
    if len(shards) > 0:
        drawn = steps_of(rng, shape, shards, -0.22, 0.18) * drawn
    return jnp.clip(drawn, min=-limit, max=limit).astype(kind)


def setup_inputs(seed: int = 0) -> dict:
    arg_keys = jax.random.split(jax.random.key(seed), 8)
    tokens = centred(arg_keys[0], (TOKEN_SLOTS, MODEL_WIDTH), 1.0, 6.0, ((0, 128),))
    frozen_value_weight = centred(arg_keys[1], (MODEL_WIDTH, VALUE_WIDTH), MODEL_WIDTH ** -0.5, 0.0625, ((0, 16),))
    adapter_down_weight = centred(arg_keys[2], (ADAPTER_COUNT, MODEL_WIDTH, ADAPTER_RANK), MODEL_WIDTH ** -0.5, 0.0625, ((0, 8), (1, 16)))
    adapter_up_weight = centred(arg_keys[3], (ADAPTER_COUNT, ADAPTER_RANK, VALUE_WIDTH), ADAPTER_RANK ** -0.5, 0.75, ((0, 8), (2, 16)))
    output_gradient = centred(arg_keys[4], (TOKEN_SLOTS, VALUE_WIDTH), 1.0, 6.0, ((0, 128),))
    adapter_per_block = draw_adapter_per_block(jax.random.fold_in(arg_keys[7], 71), 0)
    block_live_count = set_ends(jax.random.randint(arg_keys[6], (N_BLOCKS,), 1, BLOCK + 1), jax.random.fold_in(arg_keys[6], 1), 1, BLOCK).astype(jnp.int32)
    return {"tokens": tokens, "frozen_value_weight": frozen_value_weight, "adapter_down_weight": adapter_down_weight, "adapter_up_weight": adapter_up_weight, "output_gradient": output_gradient, "adapter_per_block": adapter_per_block, "block_live_count": block_live_count}


adapter_scale = 0.5


def reference(tokens, frozen_value_weight, adapter_down_weight, adapter_up_weight, output_gradient, adapter_per_block, block_live_count):
    frozen_output = jnp.dot(tokens, frozen_value_weight, preferred_element_type=jnp.float32)
    frozen_gradient = lax.dot_general(output_gradient, frozen_value_weight, (((1,), (1,)), ((), ())), preferred_element_type=jnp.float32)
    per_dev = TOK_DEV // BLOCK
    groups = N_BLOCKS // per_dev
    input_per_block = tokens.reshape(groups, per_dev, BLOCK, MODEL_WIDTH)
    dy_blocks = output_gradient.reshape(groups, per_dev, BLOCK, VALUE_WIDTH)
    ids = adapter_per_block.reshape(groups, per_dev)
    fills = block_live_count.reshape(groups, per_dev)
    positions = jnp.arange(BLOCK, dtype=jnp.int32)
    catalog = jnp.arange(ADAPTER_COUNT, dtype=jnp.int32)

    def one_device(carry, inputs):
        down_gradient_sum, up_gradient_sum = carry
        x_dev, dy_dev, adapter_index_local, fill_dev = inputs
        live_slot_mask = (positions[None, :] < fill_dev[:, None]).astype(jnp.float32)[:, :, None]
        down_per_block = adapter_down_weight[adapter_index_local].astype(jnp.float32)
        up_per_block = adapter_up_weight[adapter_index_local].astype(jnp.float32)
        input_gathered = x_dev.astype(jnp.float32)
        dy_wide = dy_dev.astype(jnp.float32)
        reduced_down_output = (jnp.einsum('gzq,gqx->gzx', input_gathered, down_per_block) * live_slot_mask).astype(jnp.bfloat16)
        reduced_output_gradient = (jnp.einsum('bkc,brc->bkr', dy_wide, up_per_block) * live_slot_mask).astype(jnp.bfloat16)
        raised_rows = jnp.einsum('bkr,brc->bkc', reduced_down_output.astype(jnp.float32), up_per_block).astype(jnp.bfloat16)
        collected_rows = jnp.einsum('qjz,qaz->qja', reduced_output_gradient.astype(jnp.float32), down_per_block).astype(jnp.bfloat16)
        choose = (adapter_index_local[:, None] == catalog[None, :]).astype(jnp.float32)
        up_terms = jnp.einsum('bkr,bkc->brc', reduced_down_output.astype(jnp.float32), dy_wide)
        down_gradient_terms = jnp.einsum('uia,uiw->uaw', input_gathered, reduced_output_gradient.astype(jnp.float32))
        down_gradient_sum = down_gradient_sum + jnp.einsum('ba,bdr->adr', choose, down_gradient_terms, precision=lax.Precision.HIGHEST)
        up_gradient_sum = up_gradient_sum + jnp.einsum('ba,brc->arc', choose, up_terms, precision=lax.Precision.HIGHEST)
        return (down_gradient_sum, up_gradient_sum), (raised_rows, collected_rows)

    start = (jnp.zeros((ADAPTER_COUNT, MODEL_WIDTH, ADAPTER_RANK), jnp.float32), jnp.zeros((ADAPTER_COUNT, ADAPTER_RANK, VALUE_WIDTH), jnp.float32))
    (down_gradient_sum, up_gradient_sum), (raised_rows, collected_rows) = lax.scan(one_device, start, (input_per_block, dy_blocks, ids, fills))
    values = (frozen_output + adapter_scale * raised_rows.reshape(TOKEN_SLOTS, VALUE_WIDTH).astype(jnp.float32)).astype(jnp.bfloat16)
    input_gradient = (frozen_gradient + adapter_scale * collected_rows.reshape(TOKEN_SLOTS, MODEL_WIDTH).astype(jnp.float32)).astype(jnp.bfloat16)
    return values, input_gradient, adapter_scale * down_gradient_sum, adapter_scale * up_gradient_sum
```

```python
import functools

import jax
import jax.numpy as jnp
from jax import lax
from jax.experimental import pallas as pl
from jax.experimental.pallas import tpu as pltpu
from jax.sharding import Mesh
from jax.sharding import PartitionSpec as P

DP = ("y", "xh")
FSDP = ("z", "xl", "c")
X = ("xh", "xl")
SCALE = 0.5
F32 = jnp.float32
BF16 = jnp.bfloat16


def nt(a, b):
    return lax.dot_general(a, b, (((1,), (1,)), ((), ())), preferred_element_type=F32)


def tn(a, b):
    return lax.dot_general(a, b, (((0,), (0,)), ((), ())), preferred_element_type=F32)


def nn(a, b):
    return jnp.dot(a, b, preferred_element_type=F32)


def shift(x, axis, by):
    return lax.ppermute(x, axis, [(i, (i + by) % 4) for i in range(4)])


def ring(x, axis):
    one, three = shift(x, axis, 1), shift(x, axis, -1)
    half = x.shape[0] // 2
    two = jnp.concatenate([shift(one[:half], axis, 1), shift(three[half:], axis, -1)], axis=0)
    return jnp.stack([x, one, two, three])


def ring_small(x, axis):
    return jnp.stack([x, shift(x, axis, 1), shift(x, axis, 2), shift(x, axis, -1)])


def live_rows(fill_ref, b, rows):
    return (lax.broadcasted_iota(jnp.int32, (rows, 1), 0) < fill_ref[b]).astype(F32)


def low_v_kernel(blocks, fill_ref, x_ref, dy_ref, up_ref, v_ref, g_ref):
    rows = dy_ref.shape[0] // blocks

    @pl.when(pl.program_id(0) == 0)
    def _():
        for b in range(blocks):
            at = pl.ds(b * rows, rows)
            up = up_ref[:, :, b].reshape(-1, up_ref.shape[-1])
            v = nn(dy_ref[at, :], up) * live_rows(fill_ref, b, rows)
            v_ref[at, :] = v.astype(BF16)

    for b in range(blocks):
        at = pl.ds(b * rows, rows)
        g_ref[0, b] = tn(v_ref[at, :], x_ref[at, :]).astype(BF16)


def low_u_kernel(blocks, steps, fill_ref, x_ref, dy_ref, down_ref, u_ref, g_ref, acc_ref):
    rows = dy_ref.shape[0] // blocks
    f = pl.program_id(0)

    @pl.when(f == 0)
    def _():
        acc_ref[...] = jnp.zeros_like(acc_ref)

    for b in range(blocks):
        at = pl.ds(b * rows, rows)
        acc_ref[at, :] += nt(x_ref[at, :], down_ref[0, 0, b])

    @pl.when(f == steps - 1)
    def _():
        for b in range(blocks):
            at = pl.ds(b * rows, rows)
            u = (acc_ref[at, :] * live_rows(fill_ref, b, rows)).astype(BF16)
            u_ref[at, :] = u
            g = tn(dy_ref[at, :], u).astype(BF16)
            g_ref[:, b] = g.reshape(g_ref.shape[0], g_ref.shape[2], g_ref.shape[3])


def base_kernel(blocks, steps, x_ref, dy_ref, w_ref, u_ref, v_ref, up_ref, down_ref, y_ref, dx_ref, acc_ref):
    rows = dy_ref.shape[0] // blocks
    f = pl.program_id(0)

    @pl.when(f == 0)
    def _():
        acc_ref[...] = jnp.zeros_like(acc_ref)

    acc_ref[...] += nn(x_ref[...], w_ref[...])
    wide = nt(dy_ref[...], w_ref[...])
    for b in range(blocks):
        at = pl.ds(b * rows, rows)
        pulled = nn(v_ref[at, :], down_ref[0, 0, b]).astype(BF16).astype(F32)
        dx_ref[at, :] = (wide[b * rows : (b + 1) * rows, :] + SCALE * pulled).astype(BF16)

    @pl.when(f == steps - 1)
    def _():
        for b in range(blocks):
            at = pl.ds(b * rows, rows)
            up = up_ref[:, :, b].reshape(-1, up_ref.shape[-1])
            lifted = nt(u_ref[at, :], up).astype(BF16).astype(F32)
            y_ref[at, :] = (acc_ref[at, :] + SCALE * lifted).astype(BF16)


def sum_kernel(members, blocks, ids_ref, g_ref, h_ref, go_ref, ho_ref, gacc_ref, hacc_ref):
    gacc_ref[...] = jnp.zeros_like(gacc_ref)
    hacc_ref[...] = jnp.zeros_like(hacc_ref)

    @pl.loop(0, members)
    def _(m):
        for b in range(blocks):
            a = ids_ref[m, b]
            gacc_ref[a] += g_ref[m, b].astype(F32)
            hacc_ref[a] += h_ref[m, b].astype(F32)

    go_ref[...] = gacc_ref[...].astype(BF16)
    ho_ref[...] = hacc_ref[...].astype(BF16)


PARAMS = pltpu.CompilerParams(vmem_limit_bytes=48 * 1024 * 1024)
VMEM = pl.BlockSpec(memory_space=pltpu.VMEM)


def whole(shape):
    zeros = (0,) * len(shape)
    return pl.BlockSpec(shape, lambda f, *_: zeros)


def body(tokens, weight, down, up, dy, ids, fill):
    rows_dev, width = tokens.shape
    value = dy.shape[1]
    blocks = ids.shape[0]
    slots, feats, rank = down.shape
    cols = up.shape[2]
    zs, xls, cs = (lax.axis_size(a) for a in FSDP)
    steps = zs * xls * cs
    adapters = slots * lax.axis_size(DP)
    x_at, y_at, xl_at = lax.axis_index(X), lax.axis_index("y"), lax.axis_index("xl")

    w_full = lax.all_gather(weight, FSDP, axis=0, tiled=True)

    ids_out = jnp.broadcast_to(jnp.pad(ids, (0, 128 - blocks)), (steps, 8, 128))
    ids_all = lax.all_to_all(ids_out, FSDP, split_axis=0, concat_axis=0, tiled=True)[:, 0, :blocks]

    up_t = jnp.swapaxes(up, 1, 2)
    up_plane = ring_small(ring_small(up_t, X), "y")
    down_t = jnp.swapaxes(down, 1, 2)
    half = slots // 2
    first = ring(jnp.moveaxis(ring_small(down_t[:half], X), 0, 0), "y")
    second = ring(ring_small(down_t[half:], "y"), X)

    mine = lax.dynamic_index_in_dim(ids_all.reshape(zs, xls, cs, blocks), xl_at, 1, keepdims=False)
    want = mine.reshape(zs * cs, 1, blocks)
    owner, slot = want // slots, want % slots
    xl_src = jnp.arange(xls, dtype=jnp.int32)[None, :, None]
    oy = (y_at - owner // 2) % 4
    ox = (x_at - (2 * (owner % 2) + xl_src)) % 4
    up_pick = up_plane.reshape(-1, cols, rank)[(oy * 4 + ox) * slots + slot]
    up_recv = lax.all_to_all(up_pick, ("z", "c"), split_axis=0, concat_axis=0, tiled=True)
    both = jnp.concatenate([first.reshape(-1, rank, feats), second.reshape(-1, rank, feats)], axis=0)
    in_first = (oy * 4 + ox) * half + slot
    in_second = first.shape[0] * first.shape[1] * half + (ox * 4 + oy) * half + slot - half
    down_pick = both[jnp.where(slot < half, in_first, in_second)]
    down_recv = lax.all_to_all(down_pick, ("z", "c"), split_axis=0, concat_axis=0, tiled=True)

    def down_at(f, *_):
        return (f // (xls * cs) * cs + f % cs, f // cs % xls, 0, 0, 0)

    up_mine = jnp.swapaxes(up_recv.reshape(zs, cs, xls, blocks, cols, rank), 1, 2)
    up_mine = up_mine.reshape(1, steps, blocks, cols, rank)

    smem = pl.BlockSpec(memory_space=pltpu.SMEM)
    x_spec = pl.BlockSpec((rows_dev, feats), lambda f, *_: (0, f))
    down_spec = pl.BlockSpec((1, 1, blocks, rank, feats), down_at)
    low_v, grad_d = pl.pallas_call(
        functools.partial(low_v_kernel, blocks),
        grid=(steps,),
        in_specs=[smem, x_spec, whole(dy.shape), whole(up_mine.shape)],
        out_specs=[whole((rows_dev, rank)), pl.BlockSpec((1, blocks, rank, feats), lambda f: (f, 0, 0, 0))],
        out_shape=[
            jax.ShapeDtypeStruct((rows_dev, rank), BF16),
            jax.ShapeDtypeStruct((steps, blocks, rank, feats), BF16),
        ],
        compiler_params=PARAMS,
        name="low_v",
    )(fill, tokens, dy, up_mine)
    grad_d = lax.all_to_all(grad_d, FSDP, split_axis=0, concat_axis=0, tiled=True)

    low_u, grad_u = pl.pallas_call(
        functools.partial(low_u_kernel, blocks, steps),
        grid=(steps,),
        in_specs=[smem, x_spec, whole(dy.shape), down_spec],
        out_specs=[whole((rows_dev, rank)), whole((steps, blocks, cols, rank))],
        out_shape=[
            jax.ShapeDtypeStruct((rows_dev, rank), BF16),
            jax.ShapeDtypeStruct((steps, blocks, cols, rank), BF16),
        ],
        scratch_shapes=[pltpu.VMEM((rows_dev, rank), F32)],
        compiler_params=PARAMS,
        name="low_u",
    )(fill, tokens, dy, down_recv)
    grad_u = lax.all_to_all(grad_u, FSDP, split_axis=0, concat_axis=0, tiled=True)

    sum_d, sum_u = pl.pallas_call(
        functools.partial(sum_kernel, steps, blocks),
        in_specs=[smem, VMEM, VMEM],
        out_specs=[VMEM, VMEM],
        out_shape=[
            jax.ShapeDtypeStruct((adapters, rank, feats), BF16),
            jax.ShapeDtypeStruct((adapters, cols, rank), BF16),
        ],
        scratch_shapes=[pltpu.VMEM((adapters, rank, feats), F32), pltpu.VMEM((adapters, cols, rank), F32)],
        compiler_params=PARAMS,
        name="sum_blocks",
    )(ids_all, grad_d, grad_u)
    part_d = lax.all_to_all(sum_d, DP, split_axis=0, concat_axis=0, tiled=True)
    part_u = lax.all_to_all(sum_u, DP, split_axis=0, concat_axis=0, tiled=True)

    values, input_gradient = pl.pallas_call(
        functools.partial(base_kernel, blocks, steps),
        grid=(steps,),
        in_specs=[
            x_spec,
            whole(dy.shape),
            pl.BlockSpec((feats, value), lambda f: (f, 0)),
            whole(low_u.shape),
            whole(low_v.shape),
            whole(up_mine.shape),
            down_spec,
        ],
        out_specs=[whole((rows_dev, value)), pl.BlockSpec((rows_dev, feats), lambda f: (0, f))],
        out_shape=[
            jax.ShapeDtypeStruct((rows_dev, value), BF16),
            jax.ShapeDtypeStruct((rows_dev, width), BF16),
        ],
        scratch_shapes=[pltpu.VMEM((rows_dev, value), F32)],
        compiler_params=PARAMS,
        name="base",
    )(tokens, dy, w_full, low_u, low_v, up_mine, down_recv)

    grad_down = SCALE * part_d.reshape(-1, slots, rank, feats).astype(F32).sum(0)
    grad_up = SCALE * part_u.reshape(-1, slots, cols, rank).astype(F32).sum(0)
    return values, input_gradient, jnp.swapaxes(grad_down, 1, 2), jnp.swapaxes(grad_up, 1, 2)


def solution(mesh):
    fine = Mesh(mesh.devices.reshape(4, 2, 4, 2, 2), DP + FSDP)
    every = DP + FSDP
    placed = (
        P(every, None),
        P(FSDP, None),
        P(DP, FSDP, None),
        P(DP, None, FSDP),
        P(every, None),
        P(every),
        P(every),
    )
    return jax.shard_map(
        body,
        mesh=fine,
        in_specs=placed,
        out_specs=(P(every, None), P(every, None), P(DP, FSDP, None), P(DP, None, FSDP)),
        check_vma=False,
    )
```

```python
import functools

import jax
import jax.numpy as jnp
from jax import lax
from jax.experimental import pallas as pl
from jax.experimental.pallas import tpu as pltpu
from jax.sharding import Mesh
from jax.sharding import PartitionSpec as P

DP = ("y", "xh")
FSDP = ("z", "xl", "c")
SCALE = 0.5
PACK = 4
F32 = jnp.float32
BF16 = jnp.bfloat16
after = lax.optimization_barrier


def nt(a, b):
    return lax.dot_general(a, b, (((1,), (1,)), ((), ())), preferred_element_type=F32)


def tn(a, b):
    return lax.dot_general(a, b, (((0,), (0,)), ((), ())), preferred_element_type=F32)


def nn(a, b):
    return jnp.dot(a, b, preferred_element_type=F32)


def shift(x, axis, by):
    n = lax.axis_size(axis)
    return lax.ppermute(x, axis, [(i, (i + by) % n) for i in range(n)])


def exchange(x, axis):
    return lax.all_to_all(x, axis, split_axis=0, concat_axis=0, tiled=True)


def live_rows(fill_ref, b, rows):
    return (lax.broadcasted_iota(jnp.int32, (rows, 1), 0) < fill_ref[b]).astype(F32)


def pack(a):
    n = a.shape[0] // PACK
    return jnp.concatenate([a[k * n : (k + 1) * n] for k in range(PACK)], axis=1)


def unpack(a):
    r = a.shape[1] // PACK
    return jnp.concatenate([a[:, k * r : (k + 1) * r] for k in range(PACK)], axis=0)


def first_kernel(blocks, per, fill_ref, x_ref, dy_ref, a_ref, v_ref, up_ref, g_ref):
    rows = dy_ref.shape[0] // blocks
    rank = v_ref.shape[1]
    half = a_ref.shape[3]
    cols = up_ref.shape[1] // a_ref.shape[0]

    @pl.when(pl.program_id(0) == 0)
    def _():
        for b in range(blocks):
            at = pl.ds(b * rows, rows)
            for f in range(a_ref.shape[0]):
                up_ref[b, pl.ds(f * cols, cols), :] = unpack(a_ref[f, b, rank:, :])
            v = nn(dy_ref[at, :], up_ref[b]) * live_rows(fill_ref, b, rows)
            v_ref[at, :] = v.astype(BF16)

    for b in range(blocks):
        at = pl.ds(b * rows, rows)
        for j in range(per):
            g_ref[j, b] = tn(v_ref[at, :], x_ref[at, pl.ds(2 * j * half, half)]).astype(BF16)


def second_kernel(blocks, per, fill_ref, x_ref, dy_ref, v_ref, a_ref, b_ref, u_ref, g_ref, acc_ref):
    rows = dy_ref.shape[0] // blocks
    rank = v_ref.shape[1]
    half = a_ref.shape[3]
    cols = dy_ref.shape[1] // a_ref.shape[0]
    step = pl.program_id(0)

    @pl.when(step == 0)
    def _():
        acc_ref[...] = jnp.zeros_like(acc_ref)

    for b in range(blocks):
        at = pl.ds(b * rows, rows)
        total = acc_ref[at, :]
        for j in range(per):
            f = step * per + j
            x_b = x_ref[at, pl.ds((2 * j + 1) * half, half)]
            total += nt(x_ref[at, pl.ds(2 * j * half, half)], a_ref[f, b, :rank, :])
            total += nt(x_b, b_ref[f, b])
            g_ref[f, b, :rank, :] = tn(v_ref[at, :], x_b).astype(BF16)
        acc_ref[at, :] = total

    @pl.when(step == pl.num_programs(0) - 1)
    def _():
        for b in range(blocks):
            at = pl.ds(b * rows, rows)
            u = (acc_ref[at, :] * live_rows(fill_ref, b, rows)).astype(BF16)
            u_ref[at, :] = u
            g = tn(dy_ref[at, :], u).astype(BF16)
            for f in range(a_ref.shape[0]):
                g_ref[f, b, rank:, :] = pack(g[f * cols : (f + 1) * cols])


def base_kernel(blocks, per, x_ref, dy_ref, w_ref, u_ref, v_ref, up_ref, a_ref, b_ref, y_ref, dx_ref, acc_ref):
    rows = dy_ref.shape[0] // blocks
    rank = v_ref.shape[1]
    half = a_ref.shape[3]
    step = pl.program_id(0)

    @pl.when(step == 0)
    def _():
        acc_ref[...] = jnp.zeros_like(acc_ref)

    acc_ref[...] += nn(x_ref[...], w_ref[...])
    wide = nt(dy_ref[...], w_ref[...])
    for b in range(blocks):
        at = pl.ds(b * rows, rows)
        v = v_ref[at, :]
        for j in range(per):
            f = step * per + j
            for k, low in ((2 * j, a_ref[f, b, :rank, :]), (2 * j + 1, b_ref[f, b])):
                pulled = nn(v, low).astype(BF16).astype(F32)
                own = wide[b * rows : (b + 1) * rows, k * half : (k + 1) * half]
                dx_ref[at, pl.ds(k * half, half)] = (own + SCALE * pulled).astype(BF16)

    @pl.when(step == pl.num_programs(0) - 1)
    def _():
        for b in range(blocks):
            at = pl.ds(b * rows, rows)
            lifted = nt(u_ref[at, :], up_ref[b]).astype(BF16).astype(F32)
            y_ref[at, :] = (acc_ref[at, :] + SCALE * lifted).astype(BF16)


def sum_kernel(ids_ref, g_ref, o_ref, acc_ref):
    members, blocks = g_ref.shape[:2]
    acc_ref[...] = jnp.zeros_like(acc_ref)

    @pl.loop(0, members)
    def _(m):
        for b in range(blocks):
            acc_ref[ids_ref[m, b]] += g_ref[m, b].astype(F32)

    o_ref[...] = acc_ref[...].astype(BF16)


PARAMS = pltpu.CompilerParams(vmem_limit_bytes=48 * 1024 * 1024)
VMEM = pl.BlockSpec(memory_space=pltpu.VMEM)
SMEM = pl.BlockSpec(memory_space=pltpu.SMEM)


def cost(flops, size):
    return pl.CostEstimate(flops=flops, bytes_accessed=size, transcendentals=0)


def whole(shape):
    zeros = (0,) * len(shape)
    return pl.BlockSpec(shape, lambda i: zeros)


def sum_blocks(ids_all, g, adapters):
    shape = (adapters,) + g.shape[2:]
    return pl.pallas_call(
        sum_kernel,
        in_specs=[SMEM, VMEM],
        out_specs=VMEM,
        out_shape=jax.ShapeDtypeStruct(shape, BF16),
        scratch_shapes=[pltpu.VMEM(shape, F32)],
        compiler_params=PARAMS,
        cost_estimate=cost(g.size, 4 * g.size),
        name="sum_blocks",
    )(ids_all, g)


def body(tokens, weight, down, up, dy, ids, fill):
    rows_dev, width = tokens.shape
    value = dy.shape[1]
    blocks = ids.shape[0]
    slots, feats, rank = down.shape
    cols = up.shape[2]
    half = feats // 2
    ys, xhs = lax.axis_size("y"), lax.axis_size("xh")
    steps = lax.axis_size(FSDP)
    adapters = slots * ys * xhs
    y_at, xh_at = lax.axis_index("y"), lax.axis_index("xh")
    up_rows = cols // PACK

    w_full = lax.all_gather(weight, FSDP, axis=0, tiled=True)

    ids_out = jnp.broadcast_to(jnp.pad(ids, (0, 128 - blocks)), (steps, 8, 128))
    ids_all = exchange(ids_out, FSDP)[:, 0, :blocks]

    down_t = jnp.swapaxes(down, 1, 2)
    up_t = jnp.swapaxes(up, 1, 2).reshape(slots, PACK, up_rows, rank)
    up_packed = jnp.swapaxes(up_t, 1, 2).reshape(slots, up_rows, PACK * rank)
    own_a = jnp.concatenate([down_t[:, :, :half], up_packed], axis=1)
    own_b = down_t[:, :, half:]

    def over_y(x):
        one, three = shift(x, "y", 1), shift(x, "y", -1)
        mid = slots // 2
        lo, hi = shift(one[:, :mid], "y", 1), shift(three[:, mid:], "y", -1)
        return jnp.stack([x, one, jnp.concatenate([lo, hi], axis=1), three])

    def over_x(x):
        return jnp.stack([x, shift(x, "xh", 1)])

    x_a = over_x(own_a)
    own_b, x_a = after((own_b, x_a))
    x_b = over_x(own_b)
    all_a = over_y(x_a)
    x_b, all_a = after((x_b, all_a))
    all_b = over_y(x_b)

    want = ids_all.reshape(steps * blocks)
    owner = want // slots
    oy, ox = (y_at - owner // xhs) % ys, (xh_at - owner % xhs) % xhs
    at = (oy * xhs + ox) * slots + want % slots

    def pick(x):
        return x.reshape(adapters, *x.shape[3:])[at].reshape(steps, blocks, *x.shape[3:])

    pick_a = pick(all_a)
    all_b, pick_a = after((all_b, pick_a))
    low_a = exchange(pick_a, FSDP)
    low_b = exchange(pick(all_b), FSDP)

    grid = 4
    per = steps // grid
    x_spec = pl.BlockSpec((rows_dev, per * feats), lambda i: (0, i))
    low_v, up_mine, grad_a = pl.pallas_call(
        functools.partial(first_kernel, blocks, per),
        grid=(grid,),
        in_specs=[SMEM, x_spec, whole(dy.shape), whole(low_a.shape)],
        out_specs=[
            whole((rows_dev, rank)),
            whole((blocks, value, rank)),
            pl.BlockSpec((per, blocks, rank, half), lambda i: (i, 0, 0, 0)),
        ],
        out_shape=[
            jax.ShapeDtypeStruct((rows_dev, rank), BF16),
            jax.ShapeDtypeStruct((blocks, value, rank), BF16),
            jax.ShapeDtypeStruct((steps, blocks, rank, half), BF16),
        ],
        compiler_params=PARAMS,
        cost_estimate=cost(rows_dev * rank * (width + 2 * value), 12 << 20),
        name="first",
    )(fill, tokens, dy, low_a)
    grad_a, low_b = after((grad_a, low_b))
    back_a = exchange(grad_a, FSDP)

    low_u, grad_b = pl.pallas_call(
        functools.partial(second_kernel, blocks, per),
        grid=(grid,),
        in_specs=[SMEM, x_spec, whole(dy.shape), whole(low_v.shape), whole(low_a.shape), whole(low_b.shape)],
        out_specs=[whole((rows_dev, rank)), whole((steps, blocks, rank + up_rows, half))],
        out_shape=[
            jax.ShapeDtypeStruct((rows_dev, rank), BF16),
            jax.ShapeDtypeStruct((steps, blocks, rank + up_rows, half), BF16),
        ],
        scratch_shapes=[pltpu.VMEM((rows_dev, rank), F32)],
        compiler_params=PARAMS,
        cost_estimate=cost(rows_dev * rank * (3 * width + 2 * value), 14 << 20),
        name="second",
    )(fill, tokens, dy, low_v, low_a, low_b)
    grad_b, back_a = after((grad_b, back_a))
    back_b = exchange(grad_b, FSDP)

    sums = jnp.concatenate(
        [sum_blocks(ids_all, back_a, adapters), sum_blocks(ids_all, back_b, adapters)], axis=1
    )
    part = exchange(sums, DP)

    grid = 8
    per = steps // grid
    x_spec = pl.BlockSpec((rows_dev, per * feats), lambda i: (0, i))
    values, input_gradient = pl.pallas_call(
        functools.partial(base_kernel, blocks, per),
        grid=(grid,),
        in_specs=[
            x_spec,
            whole(dy.shape),
            pl.BlockSpec((per * feats, value), lambda i: (i, 0)),
            whole(low_u.shape),
            whole(low_v.shape),
            whole(up_mine.shape),
            whole(low_a.shape),
            whole(low_b.shape),
        ],
        out_specs=[whole((rows_dev, value)), x_spec],
        out_shape=[
            jax.ShapeDtypeStruct((rows_dev, value), BF16),
            jax.ShapeDtypeStruct((rows_dev, width), BF16),
        ],
        scratch_shapes=[pltpu.VMEM((rows_dev, value), F32)],
        compiler_params=PARAMS,
        cost_estimate=cost(4 * rows_dev * width * value, 36 << 20),
        name="base",
    )(tokens, dy, w_full, low_u, low_v, up_mine, low_a, low_b)

    part, values, input_gradient = after((part, values, input_gradient))
    total = SCALE * part.reshape(ys * xhs, slots, -1, half).astype(F32).sum(0)
    grad_down = jnp.concatenate([total[:, :rank], total[:, rank : 2 * rank]], axis=2)
    grad_up = total[:, 2 * rank :].reshape(slots, up_rows, PACK, rank)
    grad_up = jnp.transpose(grad_up, (0, 3, 2, 1)).reshape(slots, rank, cols)
    return values, input_gradient, jnp.swapaxes(grad_down, 1, 2), grad_up


def solution(mesh):
    fine = Mesh(mesh.devices.reshape(4, 2, 4, 2, 2), DP + FSDP)
    every = DP + FSDP
    placed = (
        P(every, None),
        P(FSDP, None),
        P(DP, FSDP, None),
        P(DP, None, FSDP),
        P(every, None),
        P(every),
        P(every),
    )
    return jax.shard_map(
        body,
        mesh=fine,
        in_specs=placed,
        out_specs=(P(every, None), P(every, None), P(DP, FSDP, None), P(DP, None, FSDP)),
        check_vma=False,
    )
```

```python
import functools

import jax
import jax.numpy as jnp
from jax import lax
from jax.experimental import pallas as pl
from jax.experimental.pallas import tpu as pltpu
from jax.sharding import Mesh
from jax.sharding import PartitionSpec as P

DP = ("y", "xh")
FSDP = ("z", "xl", "c")
X = ("xh", "xl")
SCALE = 0.5
PACK = 4
F32 = jnp.float32
BF16 = jnp.bfloat16


def nt(a, b):
    return lax.dot_general(a, b, (((1,), (1,)), ((), ())), preferred_element_type=F32)


def tn(a, b):
    return lax.dot_general(a, b, (((0,), (0,)), ((), ())), preferred_element_type=F32)


def nn(a, b):
    return jnp.dot(a, b, preferred_element_type=F32)


def shift(x, axis, by):
    n = lax.axis_size(axis)
    return lax.ppermute(x, axis, [(i, (i + by) % n) for i in range(n)])


def gate(x, *needed):
    return lax.optimization_barrier((x, *needed))[0]


def exchange(x, axis):
    return lax.all_to_all(x, axis, split_axis=0, concat_axis=0, tiled=True)


def hbm(x):
    return pltpu.with_memory_space_constraint(x, pltpu.HBM)


def live_rows(fill_ref, b, rows):
    return (lax.broadcasted_iota(jnp.int32, (rows, 1), 0) < fill_ref[b]).astype(F32)


def pack(a):
    n = a.shape[0] // PACK
    return jnp.concatenate([a[k * n : (k + 1) * n] for k in range(PACK)], axis=1)


def unpack(a):
    r = a.shape[1] // PACK
    return jnp.concatenate([a[:, k * r : (k + 1) * r] for k in range(PACK)], axis=0)


def first_kernel(blocks, per, fill_ref, x_ref, dy_ref, a_ref, v_ref, up_ref, g_ref):
    rows = dy_ref.shape[0] // blocks
    rank = v_ref.shape[1]
    half = a_ref.shape[3]
    cols = up_ref.shape[1] // a_ref.shape[0]

    @pl.when(pl.program_id(0) == 0)
    def _():
        for b in range(blocks):
            at = pl.ds(b * rows, rows)
            for f in range(a_ref.shape[0]):
                up_ref[b, pl.ds(f * cols, cols), :] = unpack(a_ref[f, b, rank:, :])
            v = nn(dy_ref[at, :], up_ref[b]) * live_rows(fill_ref, b, rows)
            v_ref[at, :] = v.astype(BF16)

    for b in range(blocks):
        at = pl.ds(b * rows, rows)
        for j in range(per):
            g_ref[j, b] = tn(v_ref[at, :], x_ref[at, pl.ds(2 * j * half, half)]).astype(BF16)


def second_kernel(blocks, per, fill_ref, x_ref, dy_ref, v_ref, a_ref, b_ref, u_ref, g_ref, acc_ref):
    rows = dy_ref.shape[0] // blocks
    rank = v_ref.shape[1]
    half = a_ref.shape[3]
    cols = dy_ref.shape[1] // a_ref.shape[0]
    step = pl.program_id(0)

    @pl.when(step == 0)
    def _():
        acc_ref[...] = jnp.zeros_like(acc_ref)

    for b in range(blocks):
        at = pl.ds(b * rows, rows)
        total = acc_ref[at, :]
        for j in range(per):
            f = step * per + j
            x_b = x_ref[at, pl.ds((2 * j + 1) * half, half)]
            total += nt(x_ref[at, pl.ds(2 * j * half, half)], a_ref[f, b, :rank, :])
            total += nt(x_b, b_ref[f, b])
            g_ref[f, b, :rank, :] = tn(v_ref[at, :], x_b).astype(BF16)
        acc_ref[at, :] = total

    @pl.when(step == pl.num_programs(0) - 1)
    def _():
        for b in range(blocks):
            at = pl.ds(b * rows, rows)
            u = (acc_ref[at, :] * live_rows(fill_ref, b, rows)).astype(BF16)
            u_ref[at, :] = u
            g = tn(dy_ref[at, :], u).astype(BF16)
            for f in range(a_ref.shape[0]):
                g_ref[f, b, rank:, :] = pack(g[f * cols : (f + 1) * cols])


def base_kernel(blocks, pieces, f_ref, x_ref, dy_ref, u_ref, v_ref, up_ref, a_ref, b_ref, *refs):
    w_refs, (y_ref, dx_ref, acc_ref, w_buf, sem) = refs[:pieces], refs[pieces:]
    rows = dy_ref.shape[0] // blocks
    rank = v_ref.shape[1]
    half = a_ref.shape[3]
    step, steps = pl.program_id(0), pl.num_programs(0)
    feats = w_buf.shape[1]
    per = steps // pieces

    def fetch(i):
        for k, w_ref in enumerate(w_refs):

            @pl.when(i // per == k)
            def _():
                at = pl.ds(pl.multiple_of(i % per * feats, feats), feats)
                pltpu.make_async_copy(w_ref.at[at], w_buf.at[i % 2], sem.at[i % 2]).start()

    @pl.when(step == 0)
    def _():
        acc_ref[...] = jnp.zeros_like(acc_ref)
        fetch(step)

    @pl.when(step + 1 < steps)
    def _():
        fetch(step + 1)

    slot = step % 2
    pltpu.make_async_copy(w_refs[0].at[pl.ds(0, feats)], w_buf.at[slot], sem.at[slot]).wait()
    f = f_ref[step]
    w = w_buf[slot]
    acc_ref[...] += nn(x_ref[...], w)
    wide = nt(dy_ref[...], w)
    for b in range(blocks):
        at = pl.ds(b * rows, rows)
        v = v_ref[at, :]
        for k, low in enumerate((a_ref[f, b, :rank, :], b_ref[f, b])):
            pulled = nn(v, low).astype(BF16).astype(F32)
            own = wide[b * rows : (b + 1) * rows, k * half : (k + 1) * half]
            dx_ref[at, pl.ds(k * half, half)] = (own + SCALE * pulled).astype(BF16)

    @pl.when(step == steps - 1)
    def _():
        for b in range(blocks):
            at = pl.ds(b * rows, rows)
            lifted = nt(u_ref[at, :], up_ref[b]).astype(BF16).astype(F32)
            y_ref[at, :] = (acc_ref[at, :] + SCALE * lifted).astype(BF16)


def sum_kernel(ids_ref, to_ref, g_ref, *refs):
    members, blocks = g_ref.shape[:2]
    acc_ref = refs[-1]
    acc_ref[...] = jnp.zeros_like(acc_ref)

    @pl.loop(0, members)
    def _(m):
        for b in range(blocks):
            acc_ref[ids_ref[m, b]] += g_ref[m, b].astype(F32)

    if len(refs) == 2:
        refs[0][...] = acc_ref[...].astype(BF16)
    else:
        for k, o_ref in enumerate(refs[:-1]):
            slots = o_ref.shape[0]
            o_ref[...] = acc_ref[pl.ds(to_ref[k] * slots, slots)].astype(BF16)


def vmem(mib):
    return pltpu.CompilerParams(vmem_limit_bytes=mib * 1024 * 1024)


VMEM = pl.BlockSpec(memory_space=pltpu.VMEM)
SMEM = pl.BlockSpec(memory_space=pltpu.SMEM)


def cost(flops, size):
    return pl.CostEstimate(flops=flops, bytes_accessed=size, transcendentals=0)


def whole(shape):
    zeros = (0,) * len(shape)
    return pl.BlockSpec(shape, lambda i, *_: zeros)


def sum_blocks(ids_all, to, g, adapters, pieces):
    shape = (adapters,) + g.shape[2:]
    piece = pltpu.HBM((adapters // pieces,) + g.shape[2:], BF16)
    return pl.pallas_call(
        sum_kernel,
        in_specs=[SMEM, SMEM, VMEM],
        out_specs=[VMEM] * pieces,
        out_shape=[piece] * pieces,
        scratch_shapes=[pltpu.VMEM(shape, F32)],
        compiler_params=vmem(12),
        cost_estimate=cost(g.size, 4 * g.size),
        name="sum_blocks",
    )(ids_all, to, g)


def body(tokens, weight, down, up, dy, ids, fill):
    rows_dev, width = tokens.shape
    value = dy.shape[1]
    blocks = ids.shape[0]
    slots, feats, rank = down.shape
    cols = up.shape[2]
    half = feats // 2
    ys, xhs = lax.axis_size("y"), lax.axis_size("xh")
    steps = lax.axis_size(FSDP)
    adapters = slots * ys * xhs
    y_at, xh_at = lax.axis_index("y"), lax.axis_index("xh")
    z_at, xl_at, c_at = (lax.axis_index(a) for a in FSDP)
    up_rows = cols // PACK

    w_back, w_next = shift(weight, "z", 1), shift(weight, "z", -1)

    ids_out = jnp.broadcast_to(jnp.pad(ids, (0, 128 - blocks)), (steps, 8, 128))
    ids_all = exchange(ids_out, FSDP)[:, 0, :blocks]

    down_t = jnp.swapaxes(down, 1, 2)
    up_t = jnp.swapaxes(up, 1, 2).reshape(slots, PACK, up_rows, rank)
    up_packed = jnp.swapaxes(up_t, 1, 2).reshape(slots, up_rows, PACK * rank)
    own_a = jnp.concatenate([down_t[:, :, :half], up_packed], axis=1)
    own_b = down_t[:, :, half:]

    def over_y(x):
        one, three = shift(x, "y", 1), shift(x, "y", -1)
        mid = slots // 2
        lo, hi = shift(one[:, :mid], "y", 1), shift(three[:, mid:], "y", -1)
        return jnp.stack([x, one, jnp.concatenate([lo, hi], axis=1), three])

    def over_x(x):
        return jnp.stack([x, shift(x, "xh", 1)])

    x_a = over_x(gate(own_a, ids_out))
    all_a = over_y(x_a)

    want = ids_all.reshape(steps * blocks)
    owner = want // slots
    oy, ox = (y_at - owner // xhs) % ys, (xh_at - owner % xhs) % xhs
    at = (oy * xhs + ox) * slots + want % slots

    def pick(x):
        return x.reshape(adapters, *x.shape[3:])[at].reshape(steps, blocks, *x.shape[3:])

    pick_a = pick(gate(all_a, w_back, w_next))
    low_a = exchange(pick_a, FSDP)
    x_b = over_x(gate(own_b, x_a))
    all_b = over_y(gate(x_b, pick_a))
    pick_b = pick(all_b)
    low_b = exchange(pick_b, FSDP)

    mid = feats // 2
    w_lo = shift(gate(w_back, pick_a)[:mid], "z", 1)
    w_hi = shift(gate(w_next, pick_a)[mid:], "z", -1)
    near = jnp.concatenate([weight, w_next])
    far = jnp.concatenate([w_back, w_lo, w_hi])
    low_a, near, far = lax.optimization_barrier((low_a, near, far, pick_b))[:3]
    near_x, far_x = shift(near, X, 1), shift(far, X, -1)

    grid = 4
    per = steps // grid
    x_spec = pl.BlockSpec((rows_dev, per * feats), lambda i: (0, i))
    low_v, up_mine, grad_a = pl.pallas_call(
        functools.partial(first_kernel, blocks, per),
        grid=(grid,),
        in_specs=[SMEM, x_spec, whole(dy.shape), whole(low_a.shape)],
        out_specs=[
            whole((rows_dev, rank)),
            whole((blocks, value, rank)),
            pl.BlockSpec((per, blocks, rank, half), lambda i: (i, 0, 0, 0)),
        ],
        out_shape=[
            pltpu.HBM((rows_dev, rank), BF16),
            pltpu.HBM((blocks, value, rank), BF16),
            pltpu.HBM((steps, blocks, rank, half), BF16),
        ],
        compiler_params=vmem(16),
        cost_estimate=cost(rows_dev * rank * (width + 2 * value), 12 << 20),
        name="first",
    )(fill, hbm(tokens), hbm(dy), low_a)
    near, far = lax.optimization_barrier((near, far, low_b))[:2]
    back_a = exchange(gate(grad_a, low_b), FSDP)

    low_u, grad_b = pl.pallas_call(
        functools.partial(second_kernel, blocks, per),
        grid=(grid,),
        in_specs=[SMEM, x_spec, whole(dy.shape), whole(low_v.shape), whole(low_a.shape), whole(low_b.shape)],
        out_specs=[whole((rows_dev, rank)), whole((steps, blocks, rank + up_rows, half))],
        out_shape=[
            pltpu.HBM((rows_dev, rank), BF16),
            pltpu.HBM((steps, blocks, rank + up_rows, half), BF16),
        ],
        scratch_shapes=[pltpu.VMEM((rows_dev, rank), F32)],
        compiler_params=vmem(20),
        cost_estimate=cost(rows_dev * rank * (3 * width + 2 * value), 14 << 20),
        name="second",
    )(fill, hbm(tokens), hbm(dy), hbm(low_v), low_a, low_b)
    back_b = exchange(gate(grad_b, back_a), FSDP)
    w_own = [near, far, near_x, far_x]
    w_other = [shift(w, "c", 1) for w in (near, far, gate(near_x, low_u), gate(far_x, low_u))]
    w_all = w_own + w_other
    order = [
        (z_at + dz) % 4 * 4 + (xl_at + dx) % 2 * 2 + (c_at + dc) % 2
        for dc in (0, 1)
        for dx in (0, 1)
        for dz in (0, 1, 3, 2)
    ]

    peers = [(i, j) for i in range(ys) for j in range(xhs)]
    to = jnp.stack([(y_at + i) % ys * xhs + (xh_at + j) % xhs for i, j in peers])
    sums = sum_blocks(ids_all, to, gate(back_a, *w_other), adapters, len(peers))
    part_a = [sums[0]]
    for (i, j), piece in zip(peers[1:], sums[1:]):
        moves = [(a * xhs + b, (a + i) % ys * xhs + (b + j) % xhs) for a, b in peers]
        part_a.append(lax.ppermute(piece, DP, moves))

    values, input_gradient = pl.pallas_call(
        functools.partial(base_kernel, blocks, len(w_all)),
        grid_spec=pltpu.PrefetchScalarGridSpec(
            num_scalar_prefetch=1,
            grid=(steps,),
            in_specs=[
                pl.BlockSpec((rows_dev, feats), lambda i, f: (0, f[i])),
                whole(dy.shape),
                whole(low_u.shape),
                whole(low_v.shape),
                whole(up_mine.shape),
                whole(low_a.shape),
                whole(low_b.shape),
            ]
            + [pl.BlockSpec(memory_space=pltpu.HBM)] * len(w_all),
            out_specs=[
                whole((rows_dev, value)),
                pl.BlockSpec((rows_dev, feats), lambda i, f: (0, f[i])),
            ],
            scratch_shapes=[
                pltpu.VMEM((rows_dev, value), F32),
                pltpu.VMEM((2, feats, value), BF16),
                pltpu.SemaphoreType.DMA((2,)),
            ],
        ),
        out_shape=[pltpu.HBM((rows_dev, value), BF16), pltpu.HBM((rows_dev, width), BF16)],
        compiler_params=vmem(28),
        cost_estimate=cost(4 * rows_dev * width * value, 36 << 20),
        name="base",
    )(
        jnp.stack(order),
        *(hbm(a) for a in (tokens, dy, low_u, low_v, up_mine)),
        low_a,
        low_b,
        *(hbm(a) for a in w_all),
    )

    sum_b = sum_blocks(ids_all, to, gate(back_b, *part_a), adapters, 1)[0]
    part_b = gate(exchange(sum_b, DP), values).reshape(ys * xhs, slots, -1, half).astype(F32)
    total_a, total_b = SCALE * sum(p.astype(F32) for p in part_a), SCALE * part_b.sum(0)
    grad_down = jnp.concatenate([total_a, total_b[:, :rank]], axis=2)
    grad_up = total_b[:, rank:].reshape(slots, up_rows, PACK, rank)
    grad_up = jnp.transpose(grad_up, (0, 3, 2, 1)).reshape(slots, rank, cols)
    return values, input_gradient, jnp.swapaxes(grad_down, 1, 2), grad_up


def solution(mesh):
    fine = Mesh(mesh.devices.reshape(4, 2, 4, 2, 2), DP + FSDP)
    every = DP + FSDP
    placed = (
        P(every, None),
        P(FSDP, None),
        P(DP, FSDP, None),
        P(DP, None, FSDP),
        P(every, None),
        P(every),
        P(every),
    )
    return jax.shard_map(
        body,
        mesh=fine,
        in_specs=placed,
        out_specs=(P(every, None), P(every, None), P(DP, FSDP, None), P(DP, None, FSDP)),
        check_vma=False,
    )
```

```python
import functools

import jax
import jax.numpy as jnp
from jax import lax
from jax.experimental import pallas as pl
from jax.experimental.pallas import tpu as pltpu
from jax.sharding import Mesh
from jax.sharding import PartitionSpec as P

DP = ("y", "xh")
FSDP = ("z", "xl", "c")
X = ("xh", "xl")
SCALE = 0.5
F32 = jnp.float32
BF16 = jnp.bfloat16


def nt(a, b):
    return lax.dot_general(a, b, (((1,), (1,)), ((), ())), preferred_element_type=F32)


def tn(a, b):
    return lax.dot_general(a, b, (((0,), (0,)), ((), ())), preferred_element_type=F32)


def nn(a, b):
    return jnp.dot(a, b, preferred_element_type=F32)


def shift(x, axis, by):
    n = lax.axis_size(axis)
    return lax.ppermute(x, axis, [(i, (i + by) % n) for i in range(n)])


def gate(x, *needed):
    return lax.optimization_barrier((x, *needed))[0]


def exchange(x, axis):
    return lax.all_to_all(x, axis, split_axis=0, concat_axis=0, tiled=True)


def hbm(x):
    return pltpu.with_memory_space_constraint(x, pltpu.HBM)


def live_rows(fill_ref, b, rows):
    return (lax.broadcasted_iota(jnp.int32, (rows, 1), 0) < fill_ref[b]).astype(F32)


def pack(a, k):
    n = a.shape[0] // k
    return jnp.concatenate([a[i * n : (i + 1) * n] for i in range(k)], axis=1)


def unpack(a, k):
    r = a.shape[1] // k
    return jnp.concatenate([a[:, i * r : (i + 1) * r] for i in range(k)], axis=0)


def low_kernel(blocks, per, fill_ref, x_ref, dy_ref, packed_ref, down_ref, v_ref, u_ref, up_ref, g_ref, acc_ref):
    rows = dy_ref.shape[0] // blocks
    rank, feats = down_ref.shape[2:]
    steps = g_ref.shape[0]
    cols = dy_ref.shape[1] // steps
    step = pl.program_id(0)

    @pl.when(step == 0)
    def _():
        acc_ref[...] = jnp.zeros_like(acc_ref)
        for b in range(blocks):
            at = pl.ds(b * rows, rows)
            for f in range(steps):
                up_ref[b, pl.ds(f * cols, cols), :] = unpack(packed_ref[f, b], cols // packed_ref.shape[2])
            v = nn(dy_ref[at, :], up_ref[b]) * live_rows(fill_ref, b, rows)
            v_ref[at, :] = v.astype(BF16)

    for b in range(blocks):
        at = pl.ds(b * rows, rows)
        v = v_ref[at, :]
        total = acc_ref[at, :]
        for j in range(per):
            x = x_ref[at, pl.ds(j * feats, feats)]
            total += nt(x, down_ref[j, b])
            g_ref[step * per + j, b, :rank, :] = tn(v, x).astype(BF16)
        acc_ref[at, :] = total

    @pl.when(step == pl.num_programs(0) - 1)
    def _():
        for b in range(blocks):
            at = pl.ds(b * rows, rows)
            u = (acc_ref[at, :] * live_rows(fill_ref, b, rows)).astype(BF16)
            u_ref[at, :] = u
            g = tn(dy_ref[at, :], u).astype(BF16)
            for f in range(steps):
                g_ref[f, b, rank:, :] = pack(g[f * cols : (f + 1) * cols], feats // rank)


def base_kernel(blocks, pieces, f_ref, x_ref, dy_ref, u_ref, v_ref, up_ref, down_ref, *refs):
    w_refs, (y_ref, dx_ref, acc_ref, w_buf, sem) = refs[:pieces], refs[pieces:]
    rows = dy_ref.shape[0] // blocks
    step, steps = pl.program_id(0), pl.num_programs(0)
    feats = w_buf.shape[1]
    per = steps // pieces

    def fetch(i):
        for k, w_ref in enumerate(w_refs):

            @pl.when(i // per == k)
            def _():
                at = pl.ds(pl.multiple_of(i % per * feats, feats), feats)
                pltpu.make_async_copy(w_ref.at[at], w_buf.at[i % 2], sem.at[i % 2]).start()

    @pl.when(step == 0)
    def _():
        acc_ref[...] = jnp.zeros_like(acc_ref)
        fetch(step)

    @pl.when(step + 1 < steps)
    def _():
        fetch(step + 1)

    slot = step % 2
    pltpu.make_async_copy(w_refs[0].at[pl.ds(0, feats)], w_buf.at[slot], sem.at[slot]).wait()
    w = w_buf[slot]
    acc_ref[...] += nn(x_ref[...], w)
    wide = nt(dy_ref[...], w)
    for b in range(blocks):
        at = pl.ds(b * rows, rows)
        pulled = nn(v_ref[at, :], down_ref[0, b]).astype(BF16).astype(F32)
        dx_ref[at, :] = (wide[b * rows : (b + 1) * rows, :] + SCALE * pulled).astype(BF16)

    @pl.when(step == steps - 1)
    def _():
        for b in range(blocks):
            at = pl.ds(b * rows, rows)
            lifted = nt(u_ref[at, :], up_ref[b]).astype(BF16).astype(F32)
            y_ref[at, :] = (acc_ref[at, :] + SCALE * lifted).astype(BF16)


def sum_kernel(ids_ref, g_ref, o_ref, acc_ref):
    members, blocks = g_ref.shape[:2]
    acc_ref[...] = jnp.zeros_like(acc_ref)

    @pl.loop(0, members)
    def _(m):
        for b in range(blocks):
            acc_ref[ids_ref[m, b]] += g_ref[m, b].astype(F32)

    o_ref[...] = acc_ref[...].astype(BF16)


def vmem(mib):
    return pltpu.CompilerParams(vmem_limit_bytes=mib * 1024 * 1024)


VMEM = pl.BlockSpec(memory_space=pltpu.VMEM)
SMEM = pl.BlockSpec(memory_space=pltpu.SMEM)


def cost(flops, size):
    return pl.CostEstimate(flops=flops, bytes_accessed=size, transcendentals=0)


def whole(shape):
    zeros = (0,) * len(shape)
    return pl.BlockSpec(shape, lambda i, *_: zeros)


def sum_blocks(ids_all, g, adapters):
    shape = (adapters,) + g.shape[2:]
    return pl.pallas_call(
        sum_kernel,
        in_specs=[SMEM, VMEM],
        out_specs=VMEM,
        out_shape=pltpu.HBM(shape, BF16),
        scratch_shapes=[pltpu.VMEM(shape, F32)],
        compiler_params=vmem(16),
        cost_estimate=cost(g.size, 4 * g.size),
        name="sum_blocks",
    )(ids_all, g)


def body(tokens, weight, down, up, dy, ids, fill):
    rows_dev, width = tokens.shape
    value = dy.shape[1]
    blocks = ids.shape[0]
    slots, feats, rank = down.shape
    cols = up.shape[2]
    ys, xhs = lax.axis_size("y"), lax.axis_size("xh")
    steps = lax.axis_size(FSDP)
    adapters = slots * ys * xhs
    y_at, xh_at = lax.axis_index("y"), lax.axis_index("xh")
    z_at, xl_at, c_at = (lax.axis_index(a) for a in FSDP)
    w_back, w_next = shift(weight, "z", 1), shift(weight, "z", -1)
    mid = feats // 2
    w_lo, w_hi = shift(w_back[:mid], "z", 1), shift(w_next[mid:], "z", -1)

    ids_out = jnp.broadcast_to(jnp.pad(ids, (0, 128 - blocks)), (steps, 8, 128))
    ids_all = exchange(ids_out, FSDP)

    folds = feats // rank
    up_t = jnp.swapaxes(up, 1, 2).reshape(slots, folds, cols // folds, rank)
    up_packed = jnp.swapaxes(up_t, 1, 2).reshape(slots, cols // folds, feats)
    own = jnp.concatenate([jnp.swapaxes(down, 1, 2), up_packed], axis=1)
    x_all = jnp.stack([own, shift(own, "xh", 1)])
    one, three = shift(x_all, "y", 1), shift(x_all, "y", -1)
    lo, hi = shift(one[:, : slots // 2], "y", 1), shift(three[:, slots // 2 :], "y", -1)
    every = jnp.stack([x_all, one, jnp.concatenate([lo, hi], axis=1), three])

    ids_all = gate(ids_all, lo, hi)[:, 0, :blocks]
    want = ids_all.reshape(steps * blocks)
    owner = want // slots
    oy, ox = (y_at - owner // xhs) % ys, (xh_at - owner % xhs) % xhs
    at = (oy * xhs + ox) * slots + want % slots
    every = gate(every, w_lo, w_hi)
    picked = every.reshape(adapters, *own.shape[1:])[at].reshape(steps, blocks, *own.shape[1:])
    low = exchange(picked, FSDP)

    near = jnp.concatenate([gate(weight, picked), w_next])
    far = jnp.concatenate([gate(w_back, picked), w_lo, w_hi])
    across = [(0, 3), (3, 0), (1, 2), (2, 1)]
    near_x = lax.ppermute(near, X, across)
    low = gate(low, near_x)

    grid = 4
    per = steps // grid
    x_spec = pl.BlockSpec((rows_dev, per * feats), lambda i: (0, i))
    up_rows = cols // folds
    low_v, low_u, up_mine, grads = pl.pallas_call(
        functools.partial(low_kernel, blocks, per),
        grid=(grid,),
        in_specs=[
            SMEM,
            x_spec,
            whole(dy.shape),
            pl.BlockSpec((steps, blocks, up_rows, feats), lambda i: (0, 0, rank // up_rows, 0)),
            pl.BlockSpec((per, blocks, rank, feats), lambda i: (i, 0, 0, 0)),
        ],
        out_specs=[
            whole((rows_dev, rank)),
            whole((rows_dev, rank)),
            whole((blocks, value, rank)),
            whole(low.shape),
        ],
        out_shape=[
            pltpu.HBM((rows_dev, rank), BF16),
            pltpu.HBM((rows_dev, rank), BF16),
            pltpu.HBM((blocks, value, rank), BF16),
            pltpu.HBM(low.shape, BF16),
        ],
        scratch_shapes=[pltpu.VMEM((rows_dev, rank), F32)],
        compiler_params=vmem(24),
        cost_estimate=cost(rows_dev * rank * 4 * (width + value), 16 << 20),
        name="low",
    )(fill, *(hbm(a) for a in (tokens, dy, low, low)))
    far_x = lax.ppermute(gate(far, low_u), X, across)
    back = exchange(grads, FSDP)

    w_own = [near, far, near_x, far_x]
    w_other = [shift(gate(w, low_u), "c", 1) for w in w_own]
    w_all = w_own + w_other
    order = [
        (z_at + dz) % 4 * 4 + (xl_at + dx) % 2 * 2 + (c_at + dc) % 2
        for dc in (0, 1)
        for dx in (0, 1)
        for dz in (0, 1, 3, 2)
    ]


    values, input_gradient = pl.pallas_call(
        functools.partial(base_kernel, blocks, len(w_all)),
        grid_spec=pltpu.PrefetchScalarGridSpec(
            num_scalar_prefetch=1,
            grid=(steps,),
            in_specs=[
                pl.BlockSpec((rows_dev, feats), lambda i, f: (0, f[i])),
                whole(dy.shape),
                whole(low_u.shape),
                whole(low_v.shape),
                whole(up_mine.shape),
                pl.BlockSpec((1, blocks, rank, feats), lambda i, f: (f[i], 0, 0, 0)),
            ]
            + [pl.BlockSpec(memory_space=pltpu.HBM)] * len(w_all),
            out_specs=[
                whole((rows_dev, value)),
                pl.BlockSpec((rows_dev, feats), lambda i, f: (0, f[i])),
            ],
            scratch_shapes=[
                pltpu.VMEM((rows_dev, value), F32),
                pltpu.VMEM((2, feats, value), BF16),
                pltpu.SemaphoreType.DMA((2,)),
            ],
        ),
        out_shape=[pltpu.HBM((rows_dev, value), BF16), pltpu.HBM((rows_dev, width), BF16)],
        compiler_params=vmem(28),
        cost_estimate=cost(4 * rows_dev * width * value, 36 << 20),
        name="base",
    )(
        jnp.stack(order),
        *(hbm(a) for a in (tokens, dy, low_u, low_v, up_mine, low)),
        *(hbm(a) for a in w_all),
    )

    part = exchange(sum_blocks(ids_all, back, adapters), DP)
    part = gate(part, values).reshape(ys * xhs, slots, *own.shape[1:])
    total = SCALE * part.astype(F32).sum(0)
    grad_down = total[:, :rank]
    grad_up = total[:, rank:].reshape(slots, up_rows, folds, rank)
    grad_up = jnp.transpose(grad_up, (0, 3, 2, 1)).reshape(slots, rank, cols)
    return values, input_gradient, jnp.swapaxes(grad_down, 1, 2), grad_up


def solution(mesh):
    fine = Mesh(mesh.devices.reshape(4, 2, 4, 2, 2), DP + FSDP)
    every = DP + FSDP
    placed = (
        P(every, None),
        P(FSDP, None),
        P(DP, FSDP, None),
        P(DP, None, FSDP),
        P(every, None),
        P(every),
        P(every),
    )
    return jax.shard_map(
        body,
        mesh=fine,
        in_specs=placed,
        out_specs=(P(every, None), P(every, None), P(DP, FSDP, None), P(DP, None, FSDP)),
        check_vma=False,
    )
```

```python
import functools

import jax
import jax.numpy as jnp
from jax import lax
from jax.experimental import pallas as pl
from jax.experimental.pallas import tpu as pltpu
from jax.sharding import Mesh
from jax.sharding import PartitionSpec as P

DP = ("y", "xh")
FSDP = ("z", "xl", "c")
X = ("xh", "xl")
SCALE = 0.5
F32 = jnp.float32
BF16 = jnp.bfloat16


def nt(a, b):
    return lax.dot_general(a, b, (((1,), (1,)), ((), ())), preferred_element_type=F32)


def tn(a, b):
    return lax.dot_general(a, b, (((0,), (0,)), ((), ())), preferred_element_type=F32)


def nn(a, b):
    return jnp.dot(a, b, preferred_element_type=F32)


def shift(x, axis, by):
    n = lax.axis_size(axis)
    return lax.ppermute(x, axis, [(i, (i + by) % n) for i in range(n)])


def gate(x, *needed):
    return lax.optimization_barrier((x, *needed))[0]


def exchange(x, axis):
    return lax.all_to_all(x, axis, split_axis=0, concat_axis=0, tiled=True)


def hbm(x):
    return pltpu.with_memory_space_constraint(x, pltpu.HBM)


def live_rows(fill_ref, b, rows):
    return (lax.broadcasted_iota(jnp.int32, (rows, 1), 0) < fill_ref[b]).astype(F32)


def pack(a, k):
    n = a.shape[0] // k
    return jnp.concatenate([a[i * n : (i + 1) * n] for i in range(k)], axis=1)


def unpack(a, k):
    r = a.shape[1] // k
    return jnp.concatenate([a[:, i * r : (i + 1) * r] for i in range(k)], axis=0)


def low_kernel(blocks, per, fill_ref, x_ref, dy_ref, packed_ref, down_ref, v_ref, u_ref, up_ref, g_ref, acc_ref):
    rows = dy_ref.shape[0] // blocks
    rank, feats = down_ref.shape[2:]
    steps = g_ref.shape[0]
    cols = dy_ref.shape[1] // steps
    step = pl.program_id(0)

    @pl.when(step == 0)
    def _():
        acc_ref[...] = jnp.zeros_like(acc_ref)
        for b in range(blocks):
            at = pl.ds(b * rows, rows)
            for f in range(steps):
                up_ref[b, pl.ds(f * cols, cols), :] = unpack(packed_ref[f, b], cols // packed_ref.shape[2])
            v = nn(dy_ref[at, :], up_ref[b]) * live_rows(fill_ref, b, rows)
            v_ref[at, :] = v.astype(BF16)

    for b in range(blocks):
        at = pl.ds(b * rows, rows)
        v = v_ref[at, :]
        total = acc_ref[at, :]
        for j in range(per):
            x = x_ref[at, pl.ds(j * feats, feats)]
            total += nt(x, down_ref[j, b])
            g_ref[step * per + j, b, :rank, :] = tn(v, x).astype(BF16)
        acc_ref[at, :] = total

    @pl.when(step == pl.num_programs(0) - 1)
    def _():
        for b in range(blocks):
            at = pl.ds(b * rows, rows)
            u = (acc_ref[at, :] * live_rows(fill_ref, b, rows)).astype(BF16)
            u_ref[at, :] = u
            g = tn(dy_ref[at, :], u).astype(BF16)
            for f in range(steps):
                g_ref[f, b, rank:, :] = pack(g[f * cols : (f + 1) * cols], feats // rank)


def base_kernel(blocks, quarter, f_ref, x_ref, dy_ref, u_ref, v_ref, up_ref, down_ref, *refs):
    w_refs, (y_ref, dx_ref, acc_ref, w_buf, sem) = refs[:-5], refs[-5:]
    rows = dy_ref.shape[0] // blocks
    step, steps = pl.program_id(0), pl.num_programs(0)
    feats = w_buf.shape[1]
    per = steps // 2

    def fetch(i):
        slot, m = i % 2, i % per

        def start(src, k):
            to = w_buf.at[slot, pl.ds(pl.multiple_of(f_ref[steps + k], quarter), quarter)]
            pltpu.make_async_copy(src, to, sem.at[slot]).start()

        for core in range(2):
            own, x, ring, back, ahead, lo, hi = w_refs[7 * core : 7 * core + 7]
            for k, w_ref in enumerate((own, x)):

                @pl.when(i == core * per + k)
                def _():
                    pltpu.make_async_copy(w_ref, w_buf.at[slot], sem.at[slot]).start()

            @pl.when((i // per == core) & (m >= 2))
            def _():
                for k, w_ref in enumerate((ring, back, ahead)):
                    start(w_ref.at[m - 2], k)

            @pl.when((i // per == core) & (m >= 2) & (m < 5))
            def _():
                start(lo.at[m - 2], 3)

            @pl.when((i // per == core) & (m >= 5))
            def _():
                start(hi.at[m - 5], 3)

    @pl.when(step == 0)
    def _():
        acc_ref[...] = jnp.zeros_like(acc_ref)
        fetch(step)

    @pl.when(step + 1 < steps)
    def _():
        fetch(step + 1)

    slot = step % 2
    pltpu.make_async_copy(w_refs[0], w_buf.at[slot], sem.at[slot]).wait()
    w = w_buf[slot]
    acc_ref[...] += nn(x_ref[...], w)
    wide = nt(dy_ref[...], w)
    for b in range(blocks):
        at = pl.ds(b * rows, rows)
        pulled = nn(v_ref[at, :], down_ref[0, b]).astype(BF16).astype(F32)
        dx_ref[at, :] = (wide[b * rows : (b + 1) * rows, :] + SCALE * pulled).astype(BF16)

    @pl.when(step == steps - 1)
    def _():
        for b in range(blocks):
            at = pl.ds(b * rows, rows)
            lifted = nt(u_ref[at, :], up_ref[b]).astype(BF16).astype(F32)
            y_ref[at, :] = (acc_ref[at, :] + SCALE * lifted).astype(BF16)


def sum_kernel(ids_ref, g_ref, o_ref, acc_ref):
    members, blocks = g_ref.shape[:2]
    acc_ref[...] = jnp.zeros_like(acc_ref)

    @pl.loop(0, members)
    def _(m):
        for b in range(blocks):
            acc_ref[ids_ref[m, b]] += g_ref[m, b].astype(F32)

    o_ref[...] = acc_ref[...].astype(BF16)


def vmem(mib):
    return pltpu.CompilerParams(vmem_limit_bytes=mib * 1024 * 1024)


VMEM = pl.BlockSpec(memory_space=pltpu.VMEM)
SMEM = pl.BlockSpec(memory_space=pltpu.SMEM)


def cost(flops, size):
    return pl.CostEstimate(flops=flops, bytes_accessed=size, transcendentals=0)


def whole(shape):
    zeros = (0,) * len(shape)
    return pl.BlockSpec(shape, lambda i, *_: zeros)


def sum_blocks(ids_all, g, adapters):
    shape = (adapters,) + g.shape[2:]
    return pl.pallas_call(
        sum_kernel,
        in_specs=[SMEM, VMEM],
        out_specs=VMEM,
        out_shape=pltpu.HBM(shape, BF16),
        scratch_shapes=[pltpu.VMEM(shape, F32)],
        compiler_params=vmem(16),
        cost_estimate=cost(g.size, 4 * g.size),
        name="sum_blocks",
    )(ids_all, g)


def body(tokens, weight, down, up, dy, ids, fill):
    rows_dev, width = tokens.shape
    value = dy.shape[1]
    blocks = ids.shape[0]
    slots, feats, rank = down.shape
    cols = up.shape[2]
    ys, xhs = lax.axis_size("y"), lax.axis_size("xh")
    steps = lax.axis_size(FSDP)
    adapters = slots * ys * xhs
    y_at, xh_at = lax.axis_index("y"), lax.axis_index("xh")
    z_at, xl_at, c_at = (lax.axis_index(a) for a in FSDP)
    ids_out = jnp.broadcast_to(jnp.pad(ids, (0, 128 - blocks)), (steps, 8, 128))
    ids_all = exchange(ids_out, FSDP)

    folds = feats // rank
    up_t = jnp.swapaxes(up, 1, 2).reshape(slots, folds, cols // folds, rank)
    up_packed = jnp.swapaxes(up_t, 1, 2).reshape(slots, cols // folds, feats)
    own = jnp.concatenate([jnp.swapaxes(down, 1, 2), up_packed], axis=1)
    x_all = jnp.stack([own, shift(own, "xh", 1)])
    one, three = shift(x_all, "y", 1), shift(x_all, "y", -1)

    w_x = lax.ppermute(gate(weight, x_all), X, [(0, 3), (3, 0), (1, 2), (2, 1)])
    quarter = feats // ys
    mine = lax.dynamic_slice_in_dim(jnp.stack([weight, w_x]), y_at * quarter, quarter, axis=1)
    mine = gate(mine, ids_all)
    z_back, z_next = shift(mine, "z", 1), shift(mine, "z", -1)

    lo = shift(gate(one, ids_all)[:, : slots // 2], "y", 1)
    hi = shift(gate(three, ids_all)[:, slots // 2 :], "y", -1)
    every = jnp.stack([x_all, one, jnp.concatenate([lo, hi], axis=1), three])

    ids_all = ids_all[:, 0, :blocks]
    want = ids_all.reshape(steps * blocks)
    owner = want // slots
    oy, ox = (y_at - owner // xhs) % ys, (xh_at - owner % xhs) % xhs
    at = (oy * xhs + ox) * slots + want % slots
    every = gate(every, z_back, z_next)
    picked = every.reshape(adapters, *own.shape[1:])[at].reshape(steps, blocks, *own.shape[1:])
    low = exchange(picked, FSDP)

    z_lo = shift(gate(z_back, picked)[:1], "z", 1)
    z_hi = shift(gate(z_next, picked)[1:], "z", -1)
    ring = jnp.concatenate([z_back, z_next, z_lo, z_hi])
    y_back, y_next = shift(ring, "y", 1), shift(ring, "y", -1)
    low = gate(low, y_back, y_next)

    grid = 4
    per = steps // grid
    x_spec = pl.BlockSpec((rows_dev, per * feats), lambda i: (0, i))
    up_rows = cols // folds
    low_v, low_u, up_mine, grads = pl.pallas_call(
        functools.partial(low_kernel, blocks, per),
        grid=(grid,),
        in_specs=[
            SMEM,
            x_spec,
            whole(dy.shape),
            pl.BlockSpec((steps, blocks, up_rows, feats), lambda i: (0, 0, rank // up_rows, 0)),
            pl.BlockSpec((per, blocks, rank, feats), lambda i: (i, 0, 0, 0)),
        ],
        out_specs=[
            whole((rows_dev, rank)),
            whole((rows_dev, rank)),
            whole((blocks, value, rank)),
            whole(low.shape),
        ],
        out_shape=[
            pltpu.HBM((rows_dev, rank), BF16),
            pltpu.HBM((rows_dev, rank), BF16),
            pltpu.HBM((blocks, value, rank), BF16),
            pltpu.HBM(low.shape, BF16),
        ],
        scratch_shapes=[pltpu.VMEM((rows_dev, rank), F32)],
        compiler_params=vmem(24),
        cost_estimate=cost(rows_dev * rank * 4 * (width + value), 16 << 20),
        name="low",
    )(fill, *(hbm(a) for a in (tokens, dy, low, low)))
    y_lo = shift(gate(y_back, low_u)[:3], "y", 1)
    y_hi = shift(gate(y_next, low_u)[3:], "y", -1)
    back = exchange(grads, FSDP)

    w_own = [weight, w_x, ring, y_back, y_next, y_lo, y_hi]
    w_all = w_own + [shift(gate(w, low_u), "c", 1) for w in w_own]
    order = [
        (z_at + dz) % 4 * 4 + (xl_at + dx) % 2 * 2 + (c_at + dc) % 2
        for dc in (0, 1)
        for dz in (0, 3, 1, 2)
        for dx in (0, 1)
    ] + [(y_at + dy) % ys * quarter for dy in (0, 3, 1, 2)]

    values, input_gradient = pl.pallas_call(
        functools.partial(base_kernel, blocks, quarter),
        grid_spec=pltpu.PrefetchScalarGridSpec(
            num_scalar_prefetch=1,
            grid=(steps,),
            in_specs=[
                pl.BlockSpec((rows_dev, feats), lambda i, f: (0, f[i])),
                whole(dy.shape),
                whole(low_u.shape),
                whole(low_v.shape),
                whole(up_mine.shape),
                pl.BlockSpec((1, blocks, rank, feats), lambda i, f: (f[i], 0, 0, 0)),
            ]
            + [pl.BlockSpec(memory_space=pltpu.HBM)] * len(w_all),
            out_specs=[
                whole((rows_dev, value)),
                pl.BlockSpec((rows_dev, feats), lambda i, f: (0, f[i])),
            ],
            scratch_shapes=[
                pltpu.VMEM((rows_dev, value), F32),
                pltpu.VMEM((2, feats, value), BF16),
                pltpu.SemaphoreType.DMA((2,)),
            ],
        ),
        out_shape=[pltpu.HBM((rows_dev, value), BF16), pltpu.HBM((rows_dev, width), BF16)],
        compiler_params=vmem(28),
        cost_estimate=cost(4 * rows_dev * width * value, 36 << 20),
        name="base",
    )(
        jnp.stack(order),
        *(hbm(a) for a in (tokens, dy, low_u, low_v, up_mine, low)),
        *(hbm(a) for a in w_all),
    )

    part = exchange(sum_blocks(ids_all, back, adapters), DP)
    part = gate(part, values).reshape(ys * xhs, slots, *own.shape[1:])
    total = SCALE * part.astype(F32).sum(0)
    grad_down = total[:, :rank]
    grad_up = total[:, rank:].reshape(slots, up_rows, folds, rank)
    grad_up = jnp.transpose(grad_up, (0, 3, 2, 1)).reshape(slots, rank, cols)
    return values, input_gradient, jnp.swapaxes(grad_down, 1, 2), grad_up


def solution(mesh):
    fine = Mesh(mesh.devices.reshape(4, 2, 4, 2, 2), DP + FSDP)
    every = DP + FSDP
    placed = (
        P(every, None),
        P(FSDP, None),
        P(DP, FSDP, None),
        P(DP, None, FSDP),
        P(every, None),
        P(every),
        P(every),
    )
    return jax.shard_map(
        body,
        mesh=fine,
        in_specs=placed,
        out_specs=(P(every, None), P(every, None), P(DP, FSDP, None), P(DP, None, FSDP)),
        check_vma=False,
    )
```

```python
import functools

import jax
import jax.numpy as jnp
from jax import lax
from jax.experimental import pallas as pl
from jax.experimental.pallas import tpu as pltpu
from jax.sharding import Mesh
from jax.sharding import PartitionSpec as P

DP = ("y", "xh")
FSDP = ("z", "xl", "c")
X = ("xh", "xl")
SCALE = 0.5
F32 = jnp.float32
BF16 = jnp.bfloat16


def nt(a, b):
    return lax.dot_general(a, b, (((1,), (1,)), ((), ())), preferred_element_type=F32)


def tn(a, b):
    return lax.dot_general(a, b, (((0,), (0,)), ((), ())), preferred_element_type=F32)


def nn(a, b):
    return jnp.dot(a, b, preferred_element_type=F32)


def shift(x, axis, by):
    n = lax.axis_size(axis)
    return lax.ppermute(x, axis, [(i, (i + by) % n) for i in range(n)])


def gate(x, *needed):
    return lax.optimization_barrier((x, *needed))[0]


def exchange(x, axis):
    return lax.all_to_all(x, axis, split_axis=0, concat_axis=0, tiled=True)


def hbm(x):
    return pltpu.with_memory_space_constraint(x, pltpu.HBM)


def live_rows(fill_ref, b, rows):
    return (lax.broadcasted_iota(jnp.int32, (rows, 1), 0) < fill_ref[b]).astype(F32)


def pack(a, k):
    n = a.shape[0] // k
    return jnp.concatenate([a[i * n : (i + 1) * n] for i in range(k)], axis=1)


def unpack(a, k):
    r = a.shape[1] // k
    return jnp.concatenate([a[:, i * r : (i + 1) * r] for i in range(k)], axis=0)


def low_kernel(blocks, per, fill_ref, x_ref, dy_ref, packed_ref, down_ref, v_ref, u_ref, up_ref, g_ref, acc_ref):
    rows = dy_ref.shape[0] // blocks
    rank, feats = down_ref.shape[2:]
    steps = g_ref.shape[0]
    cols = dy_ref.shape[1] // steps
    step = pl.program_id(0)

    @pl.when(step == 0)
    def _():
        acc_ref[...] = jnp.zeros_like(acc_ref)
        for b in range(blocks):
            at = pl.ds(b * rows, rows)
            for f in range(steps):
                up_ref[b, pl.ds(f * cols, cols), :] = unpack(packed_ref[f, b], cols // packed_ref.shape[2])
            v = nn(dy_ref[at, :], up_ref[b]) * live_rows(fill_ref, b, rows)
            v_ref[at, :] = v.astype(BF16)

    for b in range(blocks):
        at = pl.ds(b * rows, rows)
        v = v_ref[at, :]
        total = acc_ref[at, :]
        for j in range(per):
            x = x_ref[at, pl.ds(j * feats, feats)]
            total += nt(x, down_ref[j, b])
            g_ref[step * per + j, b, :rank, :] = tn(v, x).astype(BF16)
        acc_ref[at, :] = total

    @pl.when(step == pl.num_programs(0) - 1)
    def _():
        for b in range(blocks):
            at = pl.ds(b * rows, rows)
            u = (acc_ref[at, :] * live_rows(fill_ref, b, rows)).astype(BF16)
            u_ref[at, :] = u
            g = tn(dy_ref[at, :], u).astype(BF16)
            for f in range(steps):
                g_ref[f, b, rank:, :] = pack(g[f * cols : (f + 1) * cols], feats // rank)


def base_kernel(blocks, quarter, f_ref, x_ref, dy_ref, u_ref, v_ref, up_ref, down_ref, *refs):
    w_refs, (y_ref, dx_ref, acc_ref, w_buf, sem) = refs[:-5], refs[-5:]
    rows = dy_ref.shape[0] // blocks
    step, steps = pl.program_id(0), pl.num_programs(0)
    feats = w_buf.shape[1]
    per = steps // 2

    def fetch(i):
        slot, m = i % 2, i % per

        def start(src, k):
            to = w_buf.at[slot, pl.ds(pl.multiple_of(f_ref[steps + k], quarter), quarter)]
            pltpu.make_async_copy(src, to, sem.at[slot]).start()

        for core in range(2):
            own, x, ring, back, ahead, lo, hi = w_refs[7 * core : 7 * core + 7]
            for k, w_ref in enumerate((own, x)):

                @pl.when(i == core * per + k)
                def _():
                    pltpu.make_async_copy(w_ref, w_buf.at[slot], sem.at[slot]).start()

            @pl.when((i // per == core) & (m >= 2))
            def _():
                for k, w_ref in enumerate((ring, back, ahead)):
                    start(w_ref.at[m - 2], k)

            @pl.when((i // per == core) & (m >= 2) & (m < 5))
            def _():
                start(lo.at[m - 2], 3)

            @pl.when((i // per == core) & (m >= 5))
            def _():
                start(hi.at[m - 5], 3)

    @pl.when(step == 0)
    def _():
        acc_ref[...] = jnp.zeros_like(acc_ref)
        fetch(step)

    @pl.when(step + 1 < steps)
    def _():
        fetch(step + 1)

    slot = step % 2
    pltpu.make_async_copy(w_refs[0], w_buf.at[slot], sem.at[slot]).wait()
    w = w_buf[slot]
    acc_ref[...] += nn(x_ref[...], w)
    wide = nt(dy_ref[...], w)
    for b in range(blocks):
        at = pl.ds(b * rows, rows)
        pulled = nn(v_ref[at, :], down_ref[0, b]).astype(BF16).astype(F32)
        dx_ref[at, :] = (wide[b * rows : (b + 1) * rows, :] + SCALE * pulled).astype(BF16)

    @pl.when(step == steps - 1)
    def _():
        for b in range(blocks):
            at = pl.ds(b * rows, rows)
            lifted = nt(u_ref[at, :], up_ref[b]).astype(BF16).astype(F32)
            y_ref[at, :] = (acc_ref[at, :] + SCALE * lifted).astype(BF16)


def sum_kernel(ids_ref, g_ref, o_ref, acc_ref):
    members, blocks = g_ref.shape[:2]
    acc_ref[...] = jnp.zeros_like(acc_ref)

    @pl.loop(0, members)
    def _(m):
        for b in range(blocks):
            acc_ref[ids_ref[m, b]] += g_ref[m, b].astype(F32)

    o_ref[...] = acc_ref[...].astype(BF16)


def vmem(mib):
    return pltpu.CompilerParams(vmem_limit_bytes=mib * 1024 * 1024)


VMEM = pl.BlockSpec(memory_space=pltpu.VMEM)
SMEM = pl.BlockSpec(memory_space=pltpu.SMEM)


def cost(flops, size):
    return pl.CostEstimate(flops=flops, bytes_accessed=size, transcendentals=0)


def whole(shape):
    zeros = (0,) * len(shape)
    return pl.BlockSpec(shape, lambda i, *_: zeros)


def sum_blocks(ids_all, g, adapters):
    shape = (adapters,) + g.shape[2:]
    return pl.pallas_call(
        sum_kernel,
        in_specs=[SMEM, VMEM],
        out_specs=VMEM,
        out_shape=pltpu.HBM(shape, BF16),
        scratch_shapes=[pltpu.VMEM(shape, F32)],
        compiler_params=vmem(16),
        cost_estimate=cost(g.size, 4 * g.size),
        name="sum_blocks",
    )(ids_all, g)


def body(tokens, weight, down, up, dy, ids, fill):
    rows_dev, width = tokens.shape
    value = dy.shape[1]
    blocks = ids.shape[0]
    slots, feats, rank = down.shape
    cols = up.shape[2]
    ys, xhs = lax.axis_size("y"), lax.axis_size("xh")
    steps = lax.axis_size(FSDP)
    adapters = slots * ys * xhs
    y_at, xh_at = lax.axis_index("y"), lax.axis_index("xh")
    z_at, xl_at, c_at = (lax.axis_index(a) for a in FSDP)
    ids_out = jnp.broadcast_to(jnp.pad(ids, (0, 128 - blocks)), (steps, 8, 128))
    ids_all = exchange(ids_out, FSDP)

    quarter = feats // ys
    mine = lax.dynamic_slice_in_dim(weight, y_at * quarter, quarter)
    z_back, z_next = shift(mine, "z", 1), shift(mine, "z", -1)

    folds = feats // rank
    up_t = jnp.swapaxes(up, 1, 2).reshape(slots, folds, cols // folds, rank)
    up_packed = jnp.swapaxes(up_t, 1, 2).reshape(slots, cols // folds, feats)
    own = jnp.concatenate([jnp.swapaxes(down, 1, 2), up_packed], axis=1)
    x_all = jnp.stack([own, shift(own, "xh", 1)])
    one, three = shift(x_all, "y", 1), shift(x_all, "y", -1)

    across = [(0, 3), (3, 0), (1, 2), (2, 1)]
    w_x = lax.ppermute(gate(weight, x_all), X, across)
    z_lo = shift(z_back[: quarter // 2], "z", 1)
    z_hi = shift(z_next[quarter // 2 :], "z", -1)
    ring = jnp.concatenate([z_back, z_next, z_lo, z_hi]).reshape(3, quarter, value)
    ring_x = lax.ppermute(ring, X, across)

    lo = shift(gate(one, ids_all, z_back, z_next)[:, : slots // 2], "y", 1)
    hi = shift(gate(three, ids_all, z_back, z_next)[:, slots // 2 :], "y", -1)
    every = jnp.stack([x_all, one, jnp.concatenate([lo, hi], axis=1), three])

    ids_all = ids_all[:, 0, :blocks]
    want = ids_all.reshape(steps * blocks)
    owner = want // slots
    oy, ox = (y_at - owner // xhs) % ys, (xh_at - owner % xhs) % xhs
    at = (oy * xhs + ox) * slots + want % slots
    every = gate(every, w_x, ring_x)
    picked = every.reshape(adapters, *own.shape[1:])[at].reshape(steps, blocks, *own.shape[1:])
    low = exchange(picked, FSDP)

    ring = jnp.concatenate([gate(ring, picked), ring_x])
    y_back, y_next = shift(ring, "y", 1), shift(ring, "y", -1)
    low = gate(low, y_back, y_next)

    grid = 4
    per = steps // grid
    x_spec = pl.BlockSpec((rows_dev, per * feats), lambda i: (0, i))
    up_rows = cols // folds
    low_v, low_u, up_mine, grads = pl.pallas_call(
        functools.partial(low_kernel, blocks, per),
        grid=(grid,),
        in_specs=[
            SMEM,
            x_spec,
            whole(dy.shape),
            pl.BlockSpec((steps, blocks, up_rows, feats), lambda i: (0, 0, rank // up_rows, 0)),
            pl.BlockSpec((per, blocks, rank, feats), lambda i: (i, 0, 0, 0)),
        ],
        out_specs=[
            whole((rows_dev, rank)),
            whole((rows_dev, rank)),
            whole((blocks, value, rank)),
            whole(low.shape),
        ],
        out_shape=[
            pltpu.HBM((rows_dev, rank), BF16),
            pltpu.HBM((rows_dev, rank), BF16),
            pltpu.HBM((blocks, value, rank), BF16),
            pltpu.HBM(low.shape, BF16),
        ],
        scratch_shapes=[pltpu.VMEM((rows_dev, rank), F32)],
        compiler_params=vmem(24),
        cost_estimate=cost(rows_dev * rank * 4 * (width + value), 16 << 20),
        name="low",
    )(fill, *(hbm(a) for a in (tokens, dy, low, low)))
    y_lo = shift(gate(y_back, low_u)[:3], "y", 1)
    y_hi = shift(gate(y_next, low_u)[3:], "y", -1)
    back = exchange(grads, FSDP)

    w_own = [weight, w_x, ring, y_back, y_next, y_lo, y_hi]
    w_all = w_own + [shift(gate(w, low_u), "c", 1) for w in w_own]
    order = [
        (z_at + dz) % 4 * 4 + (xl_at + dx) % 2 * 2 + (c_at + dc) % 2
        for dc in (0, 1)
        for dx, dz in ((0, 0), (1, 0), (0, 3), (0, 1), (0, 2), (1, 3), (1, 1), (1, 2))
    ] + [(y_at + dy) % ys * quarter for dy in (0, 3, 1, 2)]

    values, input_gradient = pl.pallas_call(
        functools.partial(base_kernel, blocks, quarter),
        grid_spec=pltpu.PrefetchScalarGridSpec(
            num_scalar_prefetch=1,
            grid=(steps,),
            in_specs=[
                pl.BlockSpec((rows_dev, feats), lambda i, f: (0, f[i])),
                whole(dy.shape),
                whole(low_u.shape),
                whole(low_v.shape),
                whole(up_mine.shape),
                pl.BlockSpec((1, blocks, rank, feats), lambda i, f: (f[i], 0, 0, 0)),
            ]
            + [pl.BlockSpec(memory_space=pltpu.HBM)] * len(w_all),
            out_specs=[
                whole((rows_dev, value)),
                pl.BlockSpec((rows_dev, feats), lambda i, f: (0, f[i])),
            ],
            scratch_shapes=[
                pltpu.VMEM((rows_dev, value), F32),
                pltpu.VMEM((2, feats, value), BF16),
                pltpu.SemaphoreType.DMA((2,)),
            ],
        ),
        out_shape=[pltpu.HBM((rows_dev, value), BF16), pltpu.HBM((rows_dev, width), BF16)],
        compiler_params=vmem(28),
        cost_estimate=cost(4 * rows_dev * width * value, 36 << 20),
        name="base",
    )(
        jnp.stack(order),
        *(hbm(a) for a in (tokens, dy, low_u, low_v, up_mine, low)),
        *(hbm(a) for a in w_all),
    )

    part = exchange(sum_blocks(ids_all, back, adapters), DP)
    part = gate(part, values).reshape(ys * xhs, slots, *own.shape[1:])
    total = SCALE * part.astype(F32).sum(0)
    grad_down = total[:, :rank]
    grad_up = total[:, rank:].reshape(slots, up_rows, folds, rank)
    grad_up = jnp.transpose(grad_up, (0, 3, 2, 1)).reshape(slots, rank, cols)
    return values, input_gradient, jnp.swapaxes(grad_down, 1, 2), grad_up


def solution(mesh):
    fine = Mesh(mesh.devices.reshape(4, 2, 4, 2, 2), DP + FSDP)
    every = DP + FSDP
    placed = (
        P(every, None),
        P(FSDP, None),
        P(DP, FSDP, None),
        P(DP, None, FSDP),
        P(every, None),
        P(every),
        P(every),
    )
    return jax.shard_map(
        body,
        mesh=fine,
        in_specs=placed,
        out_specs=(P(every, None), P(every, None), P(DP, FSDP, None), P(DP, None, FSDP)),
        check_vma=False,
    )
```

```python
import functools

import jax
import jax.numpy as jnp
from jax import lax
from jax.experimental import pallas as pl
from jax.experimental.pallas import tpu as pltpu
from jax.sharding import Mesh
from jax.sharding import PartitionSpec as P

DP = ("y", "xh")
FSDP = ("z", "xl", "c")
X = ("xh", "xl")
SCALE = 0.5
F32 = jnp.float32
BF16 = jnp.bfloat16


def nt(a, b):
    return lax.dot_general(a, b, (((1,), (1,)), ((), ())), preferred_element_type=F32)


def tn(a, b):
    return lax.dot_general(a, b, (((0,), (0,)), ((), ())), preferred_element_type=F32)


def nn(a, b):
    return jnp.dot(a, b, preferred_element_type=F32)


def shift(x, axis, by):
    n = lax.axis_size(axis)
    return lax.ppermute(x, axis, [(i, (i + by) % n) for i in range(n)])


def gate(x, *needed):
    return lax.optimization_barrier((x, *needed))[0]


def exchange(x, axis):
    return lax.all_to_all(x, axis, split_axis=0, concat_axis=0, tiled=True)


def hbm(x):
    return pltpu.with_memory_space_constraint(x, pltpu.HBM)


def live_rows(fill_ref, b, rows):
    return (lax.broadcasted_iota(jnp.int32, (rows, 1), 0) < fill_ref[b]).astype(F32)


def pack(a, k):
    n = a.shape[0] // k
    return jnp.concatenate([a[i * n : (i + 1) * n] for i in range(k)], axis=1)


def unpack(a, k):
    r = a.shape[1] // k
    return jnp.concatenate([a[:, i * r : (i + 1) * r] for i in range(k)], axis=0)


def low_kernel(blocks, per, fill_ref, x_ref, dy_ref, packed_ref, down_ref, v_ref, u_ref, up_ref, g_ref, acc_ref):
    rows = dy_ref.shape[0] // blocks
    rank, feats = down_ref.shape[2:]
    steps = g_ref.shape[0]
    cols = dy_ref.shape[1] // steps
    step = pl.program_id(0)

    @pl.when(step == 0)
    def _():
        acc_ref[...] = jnp.zeros_like(acc_ref)
        for b in range(blocks):
            at = pl.ds(b * rows, rows)
            for f in range(steps):
                up_ref[b, pl.ds(f * cols, cols), :] = unpack(packed_ref[f, b], cols // packed_ref.shape[2])
            v = nn(dy_ref[at, :], up_ref[b]) * live_rows(fill_ref, b, rows)
            v_ref[at, :] = v.astype(BF16)

    for b in range(blocks):
        at = pl.ds(b * rows, rows)
        v = v_ref[at, :]
        total = acc_ref[at, :]
        for j in range(per):
            x = x_ref[at, pl.ds(j * feats, feats)]
            total += nt(x, down_ref[j, b])
            g_ref[step * per + j, b, :rank, :] = tn(v, x).astype(BF16)
        acc_ref[at, :] = total

    @pl.when(step == pl.num_programs(0) - 1)
    def _():
        for b in range(blocks):
            at = pl.ds(b * rows, rows)
            u = (acc_ref[at, :] * live_rows(fill_ref, b, rows)).astype(BF16)
            u_ref[at, :] = u
            g = tn(dy_ref[at, :], u).astype(BF16)
            for f in range(steps):
                g_ref[f, b, rank:, :] = pack(g[f * cols : (f + 1) * cols], feats // rank)


def base_kernel(blocks, quarter, f_ref, x_ref, dy_ref, u_ref, v_ref, up_ref, down_ref, *refs):
    w_refs, (y_ref, dx_ref, acc_ref, w_buf, sem) = refs[:-5], refs[-5:]
    rows = dy_ref.shape[0] // blocks
    step, steps = pl.program_id(0), pl.num_programs(0)
    feats = w_buf.shape[1]
    per = steps // 2

    def fetch(i):
        slot, m = i % 2, i % per

        def start(src, k):
            to = w_buf.at[slot, pl.ds(pl.multiple_of(f_ref[steps + k], quarter), quarter)]
            pltpu.make_async_copy(src, to, sem.at[slot]).start()

        for core in range(2):
            own, x, ring, back, ahead, lo, hi = w_refs[7 * core : 7 * core + 7]
            for k, w_ref in enumerate((own, x)):

                @pl.when(i == core * per + k)
                def _():
                    pltpu.make_async_copy(w_ref, w_buf.at[slot], sem.at[slot]).start()

            @pl.when((i // per == core) & (m >= 2))
            def _():
                for k, w_ref in enumerate((ring, back, ahead)):
                    start(w_ref.at[m - 2], k)

            @pl.when((i // per == core) & (m >= 2) & (m < 5))
            def _():
                start(lo.at[m - 2], 3)

            @pl.when((i // per == core) & (m >= 5))
            def _():
                start(hi.at[m - 5], 3)

    @pl.when(step == 0)
    def _():
        acc_ref[...] = jnp.zeros_like(acc_ref)
        fetch(step)

    @pl.when(step + 1 < steps)
    def _():
        fetch(step + 1)

    slot = step % 2
    pltpu.make_async_copy(w_refs[0], w_buf.at[slot], sem.at[slot]).wait()
    w = w_buf[slot]
    acc_ref[...] += nn(x_ref[...], w)
    wide = nt(dy_ref[...], w)
    for b in range(blocks):
        at = pl.ds(b * rows, rows)
        pulled = nn(v_ref[at, :], down_ref[0, b]).astype(BF16).astype(F32)
        dx_ref[at, :] = (wide[b * rows : (b + 1) * rows, :] + SCALE * pulled).astype(BF16)

    @pl.when(step == steps - 1)
    def _():
        for b in range(blocks):
            at = pl.ds(b * rows, rows)
            lifted = nt(u_ref[at, :], up_ref[b]).astype(BF16).astype(F32)
            y_ref[at, :] = (acc_ref[at, :] + SCALE * lifted).astype(BF16)


def sum_kernel(ids_ref, g_ref, o_ref, acc_ref):
    members, blocks = g_ref.shape[:2]
    acc_ref[...] = jnp.zeros_like(acc_ref)

    @pl.loop(0, members)
    def _(m):
        for b in range(blocks):
            acc_ref[ids_ref[m, b]] += g_ref[m, b].astype(F32)

    o_ref[...] = acc_ref[...].astype(BF16)


def vmem(mib):
    return pltpu.CompilerParams(vmem_limit_bytes=mib * 1024 * 1024)


VMEM = pl.BlockSpec(memory_space=pltpu.VMEM)
SMEM = pl.BlockSpec(memory_space=pltpu.SMEM)


def cost(flops, size):
    return pl.CostEstimate(flops=flops, bytes_accessed=size, transcendentals=0)


def whole(shape):
    zeros = (0,) * len(shape)
    return pl.BlockSpec(shape, lambda i, *_: zeros)


def sum_blocks(ids_all, g, adapters):
    shape = (adapters,) + g.shape[2:]
    return pl.pallas_call(
        sum_kernel,
        in_specs=[SMEM, VMEM],
        out_specs=VMEM,
        out_shape=pltpu.HBM(shape, BF16),
        scratch_shapes=[pltpu.VMEM(shape, F32)],
        compiler_params=vmem(16),
        cost_estimate=cost(g.size, 4 * g.size),
        name="sum_blocks",
    )(ids_all, g)


def body(tokens, weight, down, up, dy, ids, fill):
    rows_dev, width = tokens.shape
    value = dy.shape[1]
    blocks = ids.shape[0]
    slots, feats, rank = down.shape
    cols = up.shape[2]
    ys, xhs = lax.axis_size("y"), lax.axis_size("xh")
    steps = lax.axis_size(FSDP)
    adapters = slots * ys * xhs
    y_at, xh_at = lax.axis_index("y"), lax.axis_index("xh")
    z_at, xl_at, c_at = (lax.axis_index(a) for a in FSDP)
    ids_out = jnp.broadcast_to(jnp.pad(ids, (0, 128 - blocks)), (steps, 8, 128))
    ids_all = exchange(ids_out, FSDP)

    quarter = feats // ys
    mine = lax.dynamic_slice_in_dim(weight, y_at * quarter, quarter)
    mine = gate(mine, ids_all)
    z_back, z_next = shift(mine, "z", 1), shift(mine, "z", -1)

    folds = feats // rank
    up_t = jnp.swapaxes(up, 1, 2).reshape(slots, folds, cols // folds, rank)
    up_packed = jnp.swapaxes(up_t, 1, 2).reshape(slots, cols // folds, feats)
    own = jnp.concatenate([jnp.swapaxes(down, 1, 2), up_packed], axis=1)
    x_all = jnp.stack([own, shift(own, "xh", 1)])
    one, three = shift(x_all, "y", 1), shift(x_all, "y", -1)

    across = [(0, 3), (3, 0), (1, 2), (2, 1)]
    w_x = lax.ppermute(gate(weight, x_all), X, across)
    z_lo = shift(z_back[: quarter // 2], "z", 1)
    z_hi = shift(z_next[quarter // 2 :], "z", -1)
    ring = jnp.concatenate([z_back, z_next, z_lo, z_hi]).reshape(3, quarter, value)
    ring_x = lax.ppermute(ring, X, across)

    lo = shift(gate(one, ids_all)[:, : slots // 2], "y", 1)
    hi = shift(gate(three, ids_all)[:, slots // 2 :], "y", -1)
    every = jnp.stack([x_all, one, jnp.concatenate([lo, hi], axis=1), three])

    ids_all = ids_all[:, 0, :blocks]
    want = ids_all.reshape(steps * blocks)
    owner = want // slots
    oy, ox = (y_at - owner // xhs) % ys, (xh_at - owner % xhs) % xhs
    at = (oy * xhs + ox) * slots + want % slots
    every = gate(every, z_lo, z_hi)
    picked = every.reshape(adapters, *own.shape[1:])[at].reshape(steps, blocks, *own.shape[1:])
    low = exchange(picked, FSDP)

    ring = jnp.concatenate([gate(ring, picked), ring_x])
    y_back, y_next = shift(ring, "y", 1), shift(ring, "y", -1)

    grid = 4
    per = steps // grid
    x_spec = pl.BlockSpec((rows_dev, per * feats), lambda i: (0, i))
    up_rows = cols // folds
    low_v, low_u, up_mine, grads = pl.pallas_call(
        functools.partial(low_kernel, blocks, per),
        grid=(grid,),
        in_specs=[
            SMEM,
            x_spec,
            whole(dy.shape),
            pl.BlockSpec((steps, blocks, up_rows, feats), lambda i: (0, 0, rank // up_rows, 0)),
            pl.BlockSpec((per, blocks, rank, feats), lambda i: (i, 0, 0, 0)),
        ],
        out_specs=[
            whole((rows_dev, rank)),
            whole((rows_dev, rank)),
            whole((blocks, value, rank)),
            whole(low.shape),
        ],
        out_shape=[
            pltpu.HBM((rows_dev, rank), BF16),
            pltpu.HBM((rows_dev, rank), BF16),
            pltpu.HBM((blocks, value, rank), BF16),
            pltpu.HBM(low.shape, BF16),
        ],
        scratch_shapes=[pltpu.VMEM((rows_dev, rank), F32)],
        compiler_params=vmem(24),
        cost_estimate=cost(rows_dev * rank * 4 * (width + value), 16 << 20),
        name="low",
    )(fill, *(hbm(a) for a in (tokens, dy, low, low)))
    y_lo = shift(gate(y_back, low_u)[:3], "y", 1)
    y_hi = shift(gate(y_next, low_u)[3:], "y", -1)
    back = exchange(gate(grads, y_back, y_next), FSDP)

    w_own = [weight, w_x, ring, y_back, y_next, y_lo, y_hi]
    w_all = w_own + [shift(gate(w, low_u), "c", 1) for w in w_own]
    order = [
        (z_at + dz) % 4 * 4 + (xl_at + dx) % 2 * 2 + (c_at + dc) % 2
        for dc in (0, 1)
        for dx, dz in ((0, 0), (1, 0), (0, 3), (0, 1), (0, 2), (1, 3), (1, 1), (1, 2))
    ] + [(y_at + dy) % ys * quarter for dy in (0, 3, 1, 2)]

    values, input_gradient = pl.pallas_call(
        functools.partial(base_kernel, blocks, quarter),
        grid_spec=pltpu.PrefetchScalarGridSpec(
            num_scalar_prefetch=1,
            grid=(steps,),
            in_specs=[
                pl.BlockSpec((rows_dev, feats), lambda i, f: (0, f[i])),
                whole(dy.shape),
                whole(low_u.shape),
                whole(low_v.shape),
                whole(up_mine.shape),
                pl.BlockSpec((1, blocks, rank, feats), lambda i, f: (f[i], 0, 0, 0)),
            ]
            + [pl.BlockSpec(memory_space=pltpu.HBM)] * len(w_all),
            out_specs=[
                whole((rows_dev, value)),
                pl.BlockSpec((rows_dev, feats), lambda i, f: (0, f[i])),
            ],
            scratch_shapes=[
                pltpu.VMEM((rows_dev, value), F32),
                pltpu.VMEM((2, feats, value), BF16),
                pltpu.SemaphoreType.DMA((2,)),
            ],
        ),
        out_shape=[pltpu.HBM((rows_dev, value), BF16), pltpu.HBM((rows_dev, width), BF16)],
        compiler_params=vmem(28),
        cost_estimate=cost(4 * rows_dev * width * value, 36 << 20),
        name="base",
    )(
        jnp.stack(order),
        *(hbm(a) for a in (tokens, dy, low_u, low_v, up_mine, low)),
        *(hbm(a) for a in w_all),
    )

    part = exchange(sum_blocks(ids_all, back, adapters), DP)
    part = gate(part, values).reshape(ys * xhs, slots, *own.shape[1:])
    total = SCALE * part.astype(F32).sum(0)
    grad_down = total[:, :rank]
    grad_up = total[:, rank:].reshape(slots, up_rows, folds, rank)
    grad_up = jnp.transpose(grad_up, (0, 3, 2, 1)).reshape(slots, rank, cols)
    return values, input_gradient, jnp.swapaxes(grad_down, 1, 2), grad_up


def solution(mesh):
    fine = Mesh(mesh.devices.reshape(4, 2, 4, 2, 2), DP + FSDP)
    every = DP + FSDP
    placed = (
        P(every, None),
        P(FSDP, None),
        P(DP, FSDP, None),
        P(DP, None, FSDP),
        P(every, None),
        P(every),
        P(every),
    )
    return jax.shard_map(
        body,
        mesh=fine,
        in_specs=placed,
        out_specs=(P(every, None), P(every, None), P(DP, FSDP, None), P(DP, None, FSDP)),
        check_vma=False,
    )
```

```python
import functools

import jax
import jax.numpy as jnp
from jax import lax
from jax.experimental import pallas as pl
from jax.experimental.pallas import tpu as pltpu
from jax.sharding import Mesh
from jax.sharding import PartitionSpec as P

DP = ("y", "xh")
FSDP = ("z", "xl", "c")
X = ("xh", "xl")
SCALE = 0.5
F32 = jnp.float32
BF16 = jnp.bfloat16


def nt(a, b):
    return lax.dot_general(a, b, (((1,), (1,)), ((), ())), preferred_element_type=F32)


def tn(a, b):
    return lax.dot_general(a, b, (((0,), (0,)), ((), ())), preferred_element_type=F32)


def nn(a, b):
    return jnp.dot(a, b, preferred_element_type=F32)


def shift(x, axis, by):
    n = lax.axis_size(axis)
    return lax.ppermute(x, axis, [(i, (i + by) % n) for i in range(n)])


def gate(x, *needed):
    return lax.optimization_barrier((x, *needed))[0]


def exchange(x, axis):
    return lax.all_to_all(x, axis, split_axis=0, concat_axis=0, tiled=True)


def hbm(x):
    return pltpu.with_memory_space_constraint(x, pltpu.HBM)


def live_rows(fill_ref, b, rows):
    return (lax.broadcasted_iota(jnp.int32, (rows, 1), 0) < fill_ref[b]).astype(F32)


def pack(a, k):
    n = a.shape[0] // k
    return jnp.concatenate([a[i * n : (i + 1) * n] for i in range(k)], axis=1)


def unpack(a, k):
    r = a.shape[1] // k
    return jnp.concatenate([a[:, i * r : (i + 1) * r] for i in range(k)], axis=0)


def low_kernel(blocks, per, fill_ref, x_ref, dy_ref, packed_ref, down_ref, v_ref, u_ref, up_ref, g_ref, acc_ref):
    rows = dy_ref.shape[0] // blocks
    rank, feats = down_ref.shape[2:]
    steps = g_ref.shape[0]
    cols = dy_ref.shape[1] // steps
    step = pl.program_id(0)

    @pl.when(step == 0)
    def _():
        acc_ref[...] = jnp.zeros_like(acc_ref)
        for b in range(blocks):
            at = pl.ds(b * rows, rows)
            for f in range(steps):
                up_ref[b, pl.ds(f * cols, cols), :] = unpack(packed_ref[f, b], cols // packed_ref.shape[2])
            v = nn(dy_ref[at, :], up_ref[b]) * live_rows(fill_ref, b, rows)
            v_ref[at, :] = v.astype(BF16)

    for b in range(blocks):
        at = pl.ds(b * rows, rows)
        v = v_ref[at, :]
        total = acc_ref[at, :]
        for j in range(per):
            x = x_ref[at, pl.ds(j * feats, feats)]
            total += nt(x, down_ref[j, b])
            g_ref[step * per + j, b, :rank, :] = tn(v, x).astype(BF16)
        acc_ref[at, :] = total

    @pl.when(step == pl.num_programs(0) - 1)
    def _():
        for b in range(blocks):
            at = pl.ds(b * rows, rows)
            u = (acc_ref[at, :] * live_rows(fill_ref, b, rows)).astype(BF16)
            u_ref[at, :] = u
            g = tn(dy_ref[at, :], u).astype(BF16)
            for f in range(steps):
                g_ref[f, b, rank:, :] = pack(g[f * cols : (f + 1) * cols], feats // rank)


def base_kernel(blocks, quarter, f_ref, x_ref, dy_ref, u_ref, v_ref, up_ref, down_ref, *refs):
    w_refs, (y_ref, dx_ref, acc_ref, w_buf, sem) = refs[:-5], refs[-5:]
    rows = dy_ref.shape[0] // blocks
    step, steps = pl.program_id(0), pl.num_programs(0)
    feats = w_buf.shape[1]
    per = steps // 2

    def fetch(i):
        slot, m = i % 2, i % per

        def start(src, k):
            to = w_buf.at[slot, pl.ds(pl.multiple_of(f_ref[steps + k], quarter), quarter)]
            pltpu.make_async_copy(src, to, sem.at[slot]).start()

        for core in range(2):
            own, x, ring, back, ahead, lo, hi = w_refs[7 * core : 7 * core + 7]
            for k, w_ref in enumerate((own, x)):

                @pl.when(i == core * per + k)
                def _():
                    pltpu.make_async_copy(w_ref, w_buf.at[slot], sem.at[slot]).start()

            @pl.when((i // per == core) & (m >= 2))
            def _():
                for k, w_ref in enumerate((ring, back, ahead)):
                    start(w_ref.at[m - 2], k)

            @pl.when((i // per == core) & (m >= 2) & (m < 5))
            def _():
                start(lo.at[m - 2], 3)

            @pl.when((i // per == core) & (m >= 5))
            def _():
                start(hi.at[m - 5], 3)

    @pl.when(step == 0)
    def _():
        acc_ref[...] = jnp.zeros_like(acc_ref)
        fetch(step)

    @pl.when(step + 1 < steps)
    def _():
        fetch(step + 1)

    slot = step % 2
    pltpu.make_async_copy(w_refs[0], w_buf.at[slot], sem.at[slot]).wait()
    w = w_buf[slot]
    acc_ref[...] += nn(x_ref[...], w)
    wide = nt(dy_ref[...], w)
    for b in range(blocks):
        at = pl.ds(b * rows, rows)
        pulled = nn(v_ref[at, :], down_ref[0, b]).astype(BF16).astype(F32)
        dx_ref[at, :] = (wide[b * rows : (b + 1) * rows, :] + SCALE * pulled).astype(BF16)

    @pl.when(step == steps - 1)
    def _():
        for b in range(blocks):
            at = pl.ds(b * rows, rows)
            lifted = nt(u_ref[at, :], up_ref[b]).astype(BF16).astype(F32)
            y_ref[at, :] = (acc_ref[at, :] + SCALE * lifted).astype(BF16)


def sum_kernel(ids_ref, g_ref, o_ref, acc_ref):
    members, blocks = g_ref.shape[:2]
    acc_ref[...] = jnp.zeros_like(acc_ref)

    @pl.loop(0, members)
    def _(m):
        for b in range(blocks):
            acc_ref[ids_ref[m, b]] += g_ref[m, b].astype(F32)

    o_ref[...] = acc_ref[...].astype(BF16)


def vmem(mib):
    return pltpu.CompilerParams(vmem_limit_bytes=mib * 1024 * 1024)


VMEM = pl.BlockSpec(memory_space=pltpu.VMEM)
SMEM = pl.BlockSpec(memory_space=pltpu.SMEM)


def cost(flops, size):
    return pl.CostEstimate(flops=flops, bytes_accessed=size, transcendentals=0)


def whole(shape):
    zeros = (0,) * len(shape)
    return pl.BlockSpec(shape, lambda i, *_: zeros)


def sum_blocks(ids_all, g, adapters):
    shape = (adapters,) + g.shape[2:]
    return pl.pallas_call(
        sum_kernel,
        in_specs=[SMEM, VMEM],
        out_specs=VMEM,
        out_shape=pltpu.HBM(shape, BF16),
        scratch_shapes=[pltpu.VMEM(shape, F32)],
        compiler_params=vmem(16),
        cost_estimate=cost(g.size, 4 * g.size),
        name="sum_blocks",
    )(ids_all, g)


def body(tokens, weight, down, up, dy, ids, fill):
    rows_dev, width = tokens.shape
    value = dy.shape[1]
    blocks = ids.shape[0]
    slots, feats, rank = down.shape
    cols = up.shape[2]
    ys, xhs = lax.axis_size("y"), lax.axis_size("xh")
    steps = lax.axis_size(FSDP)
    adapters = slots * ys * xhs
    y_at, xh_at = lax.axis_index("y"), lax.axis_index("xh")
    z_at, xl_at, c_at = (lax.axis_index(a) for a in FSDP)
    ids_out = jnp.broadcast_to(jnp.pad(ids, (0, 128 - blocks)), (steps, 8, 128))
    ids_all = exchange(ids_out, FSDP)

    quarter = feats // ys
    mine = lax.dynamic_slice_in_dim(weight, y_at * quarter, quarter)
    rest = [shift(mine, "z", by) for by in (1, -1, 2)]

    folds = feats // rank
    up_t = jnp.swapaxes(up, 1, 2).reshape(slots, folds, cols // folds, rank)
    up_packed = jnp.swapaxes(up_t, 1, 2).reshape(slots, cols // folds, feats)
    own = jnp.concatenate([jnp.swapaxes(down, 1, 2), up_packed], axis=1)
    x_all = jnp.stack([own, shift(own, "xh", 1)])
    one, three = shift(x_all, "y", 1), shift(x_all, "y", -1)

    across = [(0, 3), (3, 0), (1, 2), (2, 1)]
    ring = jnp.stack(rest)
    ring_x = lax.ppermute(ring, X, across)

    lo = shift(gate(one, ids_all)[:, : slots // 2], "y", 1)
    hi = shift(gate(three, ids_all)[:, slots // 2 :], "y", -1)
    every = jnp.stack([x_all, one, jnp.concatenate([lo, hi], axis=1), three])

    ids_all = ids_all[:, 0, :blocks]
    want = ids_all.reshape(steps * blocks)
    owner = want // slots
    oy, ox = (y_at - owner // xhs) % ys, (xh_at - owner % xhs) % xhs
    at = (oy * xhs + ox) * slots + want % slots
    every = gate(every, ring_x)
    picked = every.reshape(adapters, *own.shape[1:])[at].reshape(steps, blocks, *own.shape[1:])
    low = exchange(picked, FSDP)

    w_x = lax.ppermute(gate(weight, picked), X, across)
    ring = jnp.concatenate([gate(ring, picked), ring_x])
    y_back, y_next = shift(ring, "y", 1), shift(ring, "y", -1)

    grid = 4
    per = steps // grid
    x_spec = pl.BlockSpec((rows_dev, per * feats), lambda i: (0, i))
    up_rows = cols // folds
    low_v, low_u, up_mine, grads = pl.pallas_call(
        functools.partial(low_kernel, blocks, per),
        grid=(grid,),
        in_specs=[
            SMEM,
            x_spec,
            whole(dy.shape),
            pl.BlockSpec((steps, blocks, up_rows, feats), lambda i: (0, 0, rank // up_rows, 0)),
            pl.BlockSpec((per, blocks, rank, feats), lambda i: (i, 0, 0, 0)),
        ],
        out_specs=[
            whole((rows_dev, rank)),
            whole((rows_dev, rank)),
            whole((blocks, value, rank)),
            whole(low.shape),
        ],
        out_shape=[
            pltpu.HBM((rows_dev, rank), BF16),
            pltpu.HBM((rows_dev, rank), BF16),
            pltpu.HBM((blocks, value, rank), BF16),
            pltpu.HBM(low.shape, BF16),
        ],
        scratch_shapes=[pltpu.VMEM((rows_dev, rank), F32)],
        compiler_params=vmem(24),
        cost_estimate=cost(rows_dev * rank * 4 * (width + value), 16 << 20),
        name="low",
    )(fill, *(hbm(a) for a in (tokens, dy, low, low)))
    y_lo = shift(gate(y_back, low_u)[:3], "y", 1)
    y_hi = shift(gate(y_next, low_u)[3:], "y", -1)
    back = exchange(gate(grads, y_back, y_next), FSDP)

    w_own = [weight, w_x, ring, y_back, y_next, y_lo, y_hi]
    w_all = w_own + [shift(gate(w, low_u), "c", 1) for w in w_own]
    order = [
        (z_at + dz) % 4 * 4 + (xl_at + dx) % 2 * 2 + (c_at + dc) % 2
        for dc in (0, 1)
        for dx, dz in ((0, 0), (1, 0), (0, 3), (0, 1), (0, 2), (1, 3), (1, 1), (1, 2))
    ] + [(y_at + dy) % ys * quarter for dy in (0, 3, 1, 2)]

    values, input_gradient = pl.pallas_call(
        functools.partial(base_kernel, blocks, quarter),
        grid_spec=pltpu.PrefetchScalarGridSpec(
            num_scalar_prefetch=1,
            grid=(steps,),
            in_specs=[
                pl.BlockSpec((rows_dev, feats), lambda i, f: (0, f[i])),
                whole(dy.shape),
                whole(low_u.shape),
                whole(low_v.shape),
                whole(up_mine.shape),
                pl.BlockSpec((1, blocks, rank, feats), lambda i, f: (f[i], 0, 0, 0)),
            ]
            + [pl.BlockSpec(memory_space=pltpu.HBM)] * len(w_all),
            out_specs=[
                whole((rows_dev, value)),
                pl.BlockSpec((rows_dev, feats), lambda i, f: (0, f[i])),
            ],
            scratch_shapes=[
                pltpu.VMEM((rows_dev, value), F32),
                pltpu.VMEM((2, feats, value), BF16),
                pltpu.SemaphoreType.DMA((2,)),
            ],
        ),
        out_shape=[pltpu.HBM((rows_dev, value), BF16), pltpu.HBM((rows_dev, width), BF16)],
        compiler_params=vmem(28),
        cost_estimate=cost(4 * rows_dev * width * value, 36 << 20),
        name="base",
    )(
        jnp.stack(order),
        *(hbm(a) for a in (tokens, dy, low_u, low_v, up_mine, low)),
        *(hbm(a) for a in w_all),
    )

    part = exchange(sum_blocks(ids_all, back, adapters), DP)
    part = gate(part, values).reshape(ys * xhs, slots, *own.shape[1:])
    total = SCALE * part.astype(F32).sum(0)
    grad_down = total[:, :rank]
    grad_up = total[:, rank:].reshape(slots, up_rows, folds, rank)
    grad_up = jnp.transpose(grad_up, (0, 3, 2, 1)).reshape(slots, rank, cols)
    return values, input_gradient, jnp.swapaxes(grad_down, 1, 2), grad_up


def solution(mesh):
    fine = Mesh(mesh.devices.reshape(4, 2, 4, 2, 2), DP + FSDP)
    every = DP + FSDP
    placed = (
        P(every, None),
        P(FSDP, None),
        P(DP, FSDP, None),
        P(DP, None, FSDP),
        P(every, None),
        P(every),
        P(every),
    )
    return jax.shard_map(
        body,
        mesh=fine,
        in_specs=placed,
        out_specs=(P(every, None), P(every, None), P(DP, FSDP, None), P(DP, None, FSDP)),
        check_vma=False,
    )
```

```python
import functools

import jax
import jax.numpy as jnp
from jax import lax
from jax.experimental import pallas as pl
from jax.experimental.pallas import tpu as pltpu
from jax.sharding import Mesh
from jax.sharding import PartitionSpec as P

DP = ("y", "xh")
FSDP = ("z", "xl", "c")
X = ("xh", "xl")
SCALE = 0.5
F32 = jnp.float32
BF16 = jnp.bfloat16


def nt(a, b):
    return lax.dot_general(a, b, (((1,), (1,)), ((), ())), preferred_element_type=F32)


def tn(a, b):
    return lax.dot_general(a, b, (((0,), (0,)), ((), ())), preferred_element_type=F32)


def nn(a, b):
    return jnp.dot(a, b, preferred_element_type=F32)


def shift(x, axis, by):
    n = lax.axis_size(axis)
    return lax.ppermute(x, axis, [(i, (i + by) % n) for i in range(n)])


def gate(x, *needed):
    return lax.optimization_barrier((x, *needed))[0]


def exchange(x, axis):
    return lax.all_to_all(x, axis, split_axis=0, concat_axis=0, tiled=True)


def hbm(x):
    return pltpu.with_memory_space_constraint(x, pltpu.HBM)


def live_rows(fill_ref, b, rows):
    return (lax.broadcasted_iota(jnp.int32, (rows, 1), 0) < fill_ref[b]).astype(F32)


def pack(a, k):
    n = a.shape[0] // k
    return jnp.concatenate([a[i * n : (i + 1) * n] for i in range(k)], axis=1)


def unpack(a, k):
    r = a.shape[1] // k
    return jnp.concatenate([a[:, i * r : (i + 1) * r] for i in range(k)], axis=0)


def low_kernel(blocks, per, fill_ref, x_ref, dy_ref, packed_ref, down_ref, v_ref, u_ref, up_ref, g_ref, acc_ref):
    rows = dy_ref.shape[0] // blocks
    rank, feats = down_ref.shape[2:]
    steps = g_ref.shape[0]
    cols = dy_ref.shape[1] // steps
    step = pl.program_id(0)

    @pl.when(step == 0)
    def _():
        acc_ref[...] = jnp.zeros_like(acc_ref)
        for b in range(blocks):
            at = pl.ds(b * rows, rows)
            for f in range(steps):
                up_ref[b, pl.ds(f * cols, cols), :] = unpack(packed_ref[f, b], cols // packed_ref.shape[2])
            v = nn(dy_ref[at, :], up_ref[b]) * live_rows(fill_ref, b, rows)
            v_ref[at, :] = v.astype(BF16)

    for b in range(blocks):
        at = pl.ds(b * rows, rows)
        v = v_ref[at, :]
        total = acc_ref[at, :]
        for j in range(per):
            x = x_ref[at, pl.ds(j * feats, feats)]
            total += nt(x, down_ref[j, b])
            g_ref[step * per + j, b, :rank, :] = tn(v, x).astype(BF16)
        acc_ref[at, :] = total

    @pl.when(step == pl.num_programs(0) - 1)
    def _():
        for b in range(blocks):
            at = pl.ds(b * rows, rows)
            u = (acc_ref[at, :] * live_rows(fill_ref, b, rows)).astype(BF16)
            u_ref[at, :] = u
            g = tn(dy_ref[at, :], u).astype(BF16)
            for f in range(steps):
                g_ref[f, b, rank:, :] = pack(g[f * cols : (f + 1) * cols], feats // rank)


def base_kernel(blocks, quarter, f_ref, x_ref, dy_ref, u_ref, v_ref, up_ref, down_ref, *refs):
    w_refs, (y_ref, dx_ref, acc_ref, w_buf, sem) = refs[:-5], refs[-5:]
    rows = dy_ref.shape[0] // blocks
    step, steps = pl.program_id(0), pl.num_programs(0)
    feats = w_buf.shape[1]
    per = steps // 2

    def fetch(i):
        slot, m = i % 2, i % per

        def start(src, k):
            to = w_buf.at[slot, pl.ds(pl.multiple_of(f_ref[steps + k], quarter), quarter)]
            pltpu.make_async_copy(src, to, sem.at[slot]).start()

        for core in range(2):
            own, x, ring, back, ahead, lo, hi = w_refs[7 * core : 7 * core + 7]
            for k, w_ref in enumerate((own, x)):

                @pl.when(i == core * per + k)
                def _():
                    pltpu.make_async_copy(w_ref, w_buf.at[slot], sem.at[slot]).start()

            @pl.when((i // per == core) & (m >= 2))
            def _():
                for k, w_ref in enumerate((ring, back, ahead)):
                    start(w_ref.at[m - 2], k)

            @pl.when((i // per == core) & (m >= 2) & (m < 5))
            def _():
                start(lo.at[m - 2], 3)

            @pl.when((i // per == core) & (m >= 5))
            def _():
                start(hi.at[m - 5], 3)

    @pl.when(step == 0)
    def _():
        acc_ref[...] = jnp.zeros_like(acc_ref)
        fetch(step)

    @pl.when(step + 1 < steps)
    def _():
        fetch(step + 1)

    slot = step % 2
    pltpu.make_async_copy(w_refs[0], w_buf.at[slot], sem.at[slot]).wait()
    w = w_buf[slot]
    acc_ref[...] += nn(x_ref[...], w)
    wide = nt(dy_ref[...], w)
    for b in range(blocks):
        at = pl.ds(b * rows, rows)
        pulled = nn(v_ref[at, :], down_ref[0, b]).astype(BF16).astype(F32)
        dx_ref[at, :] = (wide[b * rows : (b + 1) * rows, :] + SCALE * pulled).astype(BF16)

    @pl.when(step == steps - 1)
    def _():
        for b in range(blocks):
            at = pl.ds(b * rows, rows)
            lifted = nt(u_ref[at, :], up_ref[b]).astype(BF16).astype(F32)
            y_ref[at, :] = (acc_ref[at, :] + SCALE * lifted).astype(BF16)


def sum_kernel(ids_ref, g_ref, o_ref, acc_ref):
    members, blocks = g_ref.shape[:2]
    acc_ref[...] = jnp.zeros_like(acc_ref)

    @pl.loop(0, members)
    def _(m):
        for b in range(blocks):
            acc_ref[ids_ref[m, b]] += g_ref[m, b].astype(F32)

    o_ref[...] = acc_ref[...].astype(BF16)


def pick_kernel(members, blocks, oy_ref, ox_ref, slot_ref, own_ref, one_ref, lo_ref, hi_ref, three_ref, o_ref, sem):
    mid = lo_ref.shape[1]

    @pl.loop(0, members)
    def _(m):
        for b in range(blocks):
            oy, ox, slot = oy_ref[m, b], ox_ref[m, b], slot_ref[m, b]
            for here, ref, at in (
                (oy == 0, own_ref, slot),
                (oy == 1, one_ref, slot),
                ((oy == 2) & (slot < mid), lo_ref, slot),
                ((oy == 2) & (slot >= mid), hi_ref, slot - mid),
                (oy == 3, three_ref, slot),
            ):

                @pl.when(here)
                def _():
                    pltpu.make_async_copy(ref.at[ox, at], o_ref.at[m, b], sem).start()

    pltpu.make_async_copy(o_ref, o_ref, sem).wait()


def vmem(mib):
    return pltpu.CompilerParams(vmem_limit_bytes=mib * 1024 * 1024)


VMEM = pl.BlockSpec(memory_space=pltpu.VMEM)
SMEM = pl.BlockSpec(memory_space=pltpu.SMEM)


def cost(flops, size):
    return pl.CostEstimate(flops=flops, bytes_accessed=size, transcendentals=0)


def whole(shape):
    zeros = (0,) * len(shape)
    return pl.BlockSpec(shape, lambda i, *_: zeros)


def sum_blocks(ids_all, g, adapters):
    shape = (adapters,) + g.shape[2:]
    return pl.pallas_call(
        sum_kernel,
        in_specs=[SMEM, VMEM],
        out_specs=VMEM,
        out_shape=pltpu.HBM(shape, BF16),
        scratch_shapes=[pltpu.VMEM(shape, F32)],
        compiler_params=vmem(16),
        cost_estimate=cost(g.size, 4 * g.size),
        name="sum_blocks",
    )(ids_all, g)


def body(tokens, weight, down, up, dy, ids, fill):
    rows_dev, width = tokens.shape
    value = dy.shape[1]
    blocks = ids.shape[0]
    slots, feats, rank = down.shape
    cols = up.shape[2]
    ys, xhs = lax.axis_size("y"), lax.axis_size("xh")
    steps = lax.axis_size(FSDP)
    adapters = slots * ys * xhs
    y_at, xh_at = lax.axis_index("y"), lax.axis_index("xh")
    z_at, xl_at, c_at = (lax.axis_index(a) for a in FSDP)
    ids_out = jnp.broadcast_to(jnp.pad(ids, (0, 128 - blocks)), (steps, 8, 128))
    ids_all = exchange(ids_out, FSDP)

    quarter = feats // ys
    mine = lax.dynamic_slice_in_dim(weight, y_at * quarter, quarter)
    rest = [shift(mine, "z", by) for by in (1, -1, 2)]

    folds = feats // rank
    up_t = jnp.swapaxes(up, 1, 2).reshape(slots, folds, cols // folds, rank)
    up_packed = jnp.swapaxes(up_t, 1, 2).reshape(slots, cols // folds, feats)
    own = jnp.concatenate([jnp.swapaxes(down, 1, 2), up_packed], axis=1)
    x_all = jnp.stack([own, shift(own, "xh", 1)])
    one, three = shift(x_all, "y", 1), shift(x_all, "y", -1)

    across = [(0, 3), (3, 0), (1, 2), (2, 1)]
    ring = jnp.stack(rest)
    beside = [(0, 1), (1, 0), (2, 3), (3, 2)]
    mid = quarter // 2
    ring_x = jnp.concatenate(
        [lax.ppermute(ring[:, :mid], X, across), lax.ppermute(ring[:, mid:], X, beside)], axis=1
    )

    lo = shift(gate(one, ids_all)[:, : slots // 2], "y", 1)
    hi = shift(gate(three, ids_all)[:, slots // 2 :], "y", -1)
    ids_all = ids_all[:, 0, :blocks]
    owner = ids_all // slots
    oy, ox = (y_at - owner // xhs) % ys, (xh_at - owner % xhs) % xhs
    any_spec = pl.BlockSpec(memory_space=pl.ANY)
    picked = pl.pallas_call(
        functools.partial(pick_kernel, steps, blocks),
        in_specs=[SMEM] * 3 + [any_spec] * 5,
        out_specs=any_spec,
        out_shape=pltpu.HBM((steps, blocks, *own.shape[1:]), BF16),
        scratch_shapes=[pltpu.SemaphoreType.DMA],
        compiler_params=vmem(4),
        cost_estimate=cost(0, 2 * steps * blocks * own[0].size * 2),
        name="pick",
    )(oy, ox, ids_all % slots, x_all, gate(one, ring_x), lo, hi, three)
    low = exchange(picked, FSDP)

    w_x = lax.ppermute(gate(weight, picked), X, across)
    ring = jnp.concatenate([gate(ring, picked), ring_x])
    y_back, y_next = shift(ring, "y", 1), shift(ring, "y", -1)

    grid = 4
    per = steps // grid
    x_spec = pl.BlockSpec((rows_dev, per * feats), lambda i: (0, i))
    up_rows = cols // folds
    low_v, low_u, up_mine, grads = pl.pallas_call(
        functools.partial(low_kernel, blocks, per),
        grid=(grid,),
        in_specs=[
            SMEM,
            x_spec,
            whole(dy.shape),
            pl.BlockSpec((steps, blocks, up_rows, feats), lambda i: (0, 0, rank // up_rows, 0)),
            pl.BlockSpec((per, blocks, rank, feats), lambda i: (i, 0, 0, 0)),
        ],
        out_specs=[
            whole((rows_dev, rank)),
            whole((rows_dev, rank)),
            whole((blocks, value, rank)),
            whole(low.shape),
        ],
        out_shape=[
            pltpu.HBM((rows_dev, rank), BF16),
            pltpu.HBM((rows_dev, rank), BF16),
            pltpu.HBM((blocks, value, rank), BF16),
            pltpu.HBM(low.shape, BF16),
        ],
        scratch_shapes=[pltpu.VMEM((rows_dev, rank), F32)],
        compiler_params=vmem(24),
        cost_estimate=cost(rows_dev * rank * 4 * (width + value), 16 << 20),
        name="low",
    )(fill, *(hbm(a) for a in (tokens, dy, low, low)))
    y_lo = shift(gate(y_back, low_u)[:3], "y", 1)
    y_hi = shift(gate(y_next, low_u)[3:], "y", -1)
    back = exchange(gate(grads, y_back, y_next), FSDP)

    w_own = [weight, w_x, ring, y_back, y_next, y_lo, y_hi]
    w_all = w_own + [shift(gate(w, low_u), "c", 1) for w in w_own]
    order = [
        (z_at + dz) % 4 * 4 + (xl_at + dx) % 2 * 2 + (c_at + dc) % 2
        for dc in (0, 1)
        for dx, dz in ((0, 0), (1, 0), (0, 3), (0, 1), (0, 2), (1, 3), (1, 1), (1, 2))
    ] + [(y_at + dy) % ys * quarter for dy in (0, 3, 1, 2)]

    values, input_gradient = pl.pallas_call(
        functools.partial(base_kernel, blocks, quarter),
        grid_spec=pltpu.PrefetchScalarGridSpec(
            num_scalar_prefetch=1,
            grid=(steps,),
            in_specs=[
                pl.BlockSpec((rows_dev, feats), lambda i, f: (0, f[i])),
                whole(dy.shape),
                whole(low_u.shape),
                whole(low_v.shape),
                whole(up_mine.shape),
                pl.BlockSpec((1, blocks, rank, feats), lambda i, f: (f[i], 0, 0, 0)),
            ]
            + [pl.BlockSpec(memory_space=pltpu.HBM)] * len(w_all),
            out_specs=[
                whole((rows_dev, value)),
                pl.BlockSpec((rows_dev, feats), lambda i, f: (0, f[i])),
            ],
            scratch_shapes=[
                pltpu.VMEM((rows_dev, value), F32),
                pltpu.VMEM((2, feats, value), BF16),
                pltpu.SemaphoreType.DMA((2,)),
            ],
        ),
        out_shape=[pltpu.HBM((rows_dev, value), BF16), pltpu.HBM((rows_dev, width), BF16)],
        compiler_params=vmem(28),
        cost_estimate=cost(4 * rows_dev * width * value, 36 << 20),
        name="base",
    )(
        jnp.stack(order),
        *(hbm(a) for a in (tokens, dy, low_u, low_v, up_mine, low)),
        *(hbm(a) for a in w_all),
    )

    part = exchange(sum_blocks(ids_all, back, adapters), DP)
    part = gate(part, values).reshape(ys * xhs, slots, *own.shape[1:])
    total = SCALE * part.astype(F32).sum(0)
    grad_down = total[:, :rank]
    grad_up = total[:, rank:].reshape(slots, up_rows, folds, rank)
    grad_up = jnp.transpose(grad_up, (0, 3, 2, 1)).reshape(slots, rank, cols)
    return values, input_gradient, jnp.swapaxes(grad_down, 1, 2), grad_up


def solution(mesh):
    fine = Mesh(mesh.devices.reshape(4, 2, 4, 2, 2), DP + FSDP)
    every = DP + FSDP
    placed = (
        P(every, None),
        P(FSDP, None),
        P(DP, FSDP, None),
        P(DP, None, FSDP),
        P(every, None),
        P(every),
        P(every),
    )
    return jax.shard_map(
        body,
        mesh=fine,
        in_specs=placed,
        out_specs=(P(every, None), P(every, None), P(DP, FSDP, None), P(DP, None, FSDP)),
        check_vma=False,
    )
```

```python
import functools

import jax
import jax.numpy as jnp
from jax import lax
from jax.experimental import pallas as pl
from jax.experimental.pallas import tpu as pltpu
from jax.sharding import Mesh
from jax.sharding import PartitionSpec as P

DP = ("y", "xh")
FSDP = ("z", "xl", "c")
X = ("xh", "xl")
SCALE = 0.5
F32 = jnp.float32
BF16 = jnp.bfloat16


def nt(a, b):
    return lax.dot_general(a, b, (((1,), (1,)), ((), ())), preferred_element_type=F32)


def tn(a, b):
    return lax.dot_general(a, b, (((0,), (0,)), ((), ())), preferred_element_type=F32)


def nn(a, b):
    return jnp.dot(a, b, preferred_element_type=F32)


def shift(x, axis, by):
    n = lax.axis_size(axis)
    return lax.ppermute(x, axis, [(i, (i + by) % n) for i in range(n)])


def gate(x, *needed):
    return lax.optimization_barrier((x, *needed))[0]


def exchange(x, axis):
    return lax.all_to_all(x, axis, split_axis=0, concat_axis=0, tiled=True)


def hbm(x):
    return pltpu.with_memory_space_constraint(x, pltpu.HBM)


def live_rows(fill_ref, b, rows):
    return (lax.broadcasted_iota(jnp.int32, (rows, 1), 0) < fill_ref[b]).astype(F32)


def pack(a, k):
    n = a.shape[0] // k
    return jnp.concatenate([a[i * n : (i + 1) * n] for i in range(k)], axis=1)


def unpack(a, k):
    r = a.shape[1] // k
    return jnp.concatenate([a[:, i * r : (i + 1) * r] for i in range(k)], axis=0)


def low_kernel(blocks, per, fill_ref, x_ref, dy_ref, packed_ref, down_ref, v_ref, u_ref, up_ref, g_ref, acc_ref):
    rows = dy_ref.shape[0] // blocks
    rank, feats = down_ref.shape[2:]
    steps = g_ref.shape[0]
    cols = dy_ref.shape[1] // steps
    step = pl.program_id(0)

    @pl.when(step == 0)
    def _():
        acc_ref[...] = jnp.zeros_like(acc_ref)
        for b in range(blocks):
            at = pl.ds(b * rows, rows)
            for f in range(steps):
                up_ref[b, pl.ds(f * cols, cols), :] = unpack(packed_ref[f, b], cols // packed_ref.shape[2])
            v = nn(dy_ref[at, :], up_ref[b]) * live_rows(fill_ref, b, rows)
            v_ref[at, :] = v.astype(BF16)

    for b in range(blocks):
        at = pl.ds(b * rows, rows)
        v = v_ref[at, :]
        total = acc_ref[at, :]
        for j in range(per):
            x = x_ref[at, pl.ds(j * feats, feats)]
            total += nt(x, down_ref[j, b])
            g_ref[step * per + j, b, :rank, :] = tn(v, x).astype(BF16)
        acc_ref[at, :] = total

    @pl.when(step == pl.num_programs(0) - 1)
    def _():
        for b in range(blocks):
            at = pl.ds(b * rows, rows)
            u = (acc_ref[at, :] * live_rows(fill_ref, b, rows)).astype(BF16)
            u_ref[at, :] = u
            g = tn(dy_ref[at, :], u).astype(BF16)
            for f in range(steps):
                g_ref[f, b, rank:, :] = pack(g[f * cols : (f + 1) * cols], feats // rank)


def base_kernel(blocks, quarter, f_ref, x_ref, dy_ref, u_ref, v_ref, up_ref, down_ref, *refs):
    w_refs, (y_ref, dx_ref, acc_ref, w_buf, sem) = refs[:-5], refs[-5:]
    rows = dy_ref.shape[0] // blocks
    step, steps = pl.program_id(0), pl.num_programs(0)
    feats = w_buf.shape[1]
    per = steps // 2

    def fetch(i):
        slot, m = i % 2, i % per

        def start(src, k):
            to = w_buf.at[slot, pl.ds(pl.multiple_of(f_ref[steps + k], quarter), quarter)]
            pltpu.make_async_copy(src, to, sem.at[slot]).start()

        for core in range(2):
            own, x, ring, back, ahead, lo, hi = w_refs[7 * core : 7 * core + 7]
            for k, w_ref in enumerate((own, x)):

                @pl.when(i == core * per + k)
                def _():
                    pltpu.make_async_copy(w_ref, w_buf.at[slot], sem.at[slot]).start()

            @pl.when((i // per == core) & (m >= 2))
            def _():
                for k, w_ref in enumerate((ring, back, ahead)):
                    start(w_ref.at[m - 2], k)

            @pl.when((i // per == core) & (m >= 2) & (m < 5))
            def _():
                start(lo.at[m - 2], 3)

            @pl.when((i // per == core) & (m >= 5))
            def _():
                start(hi.at[m - 5], 3)

    @pl.when(step == 0)
    def _():
        acc_ref[...] = jnp.zeros_like(acc_ref)
        fetch(step)

    @pl.when(step + 1 < steps)
    def _():
        fetch(step + 1)

    slot = step % 2
    pltpu.make_async_copy(w_refs[0], w_buf.at[slot], sem.at[slot]).wait()
    w = w_buf[slot]
    acc_ref[...] += nn(x_ref[...], w)
    wide = nt(dy_ref[...], w)
    for b in range(blocks):
        at = pl.ds(b * rows, rows)
        pulled = nn(v_ref[at, :], down_ref[0, b]).astype(BF16).astype(F32)
        dx_ref[at, :] = (wide[b * rows : (b + 1) * rows, :] + SCALE * pulled).astype(BF16)

    @pl.when(step == steps - 1)
    def _():
        for b in range(blocks):
            at = pl.ds(b * rows, rows)
            lifted = nt(u_ref[at, :], up_ref[b]).astype(BF16).astype(F32)
            y_ref[at, :] = (acc_ref[at, :] + SCALE * lifted).astype(BF16)


def sum_kernel(ids_ref, g_ref, o_ref, acc_ref):
    members, blocks = g_ref.shape[:2]
    acc_ref[...] = jnp.zeros_like(acc_ref)

    @pl.loop(0, members)
    def _(m):
        for b in range(blocks):
            acc_ref[ids_ref[m, b]] += g_ref[m, b].astype(F32)

    o_ref[...] = acc_ref[...].astype(BF16)


def vmem(mib):
    return pltpu.CompilerParams(vmem_limit_bytes=mib * 1024 * 1024)


VMEM = pl.BlockSpec(memory_space=pltpu.VMEM)
SMEM = pl.BlockSpec(memory_space=pltpu.SMEM)


def cost(flops, size):
    return pl.CostEstimate(flops=flops, bytes_accessed=size, transcendentals=0)


def whole(shape):
    zeros = (0,) * len(shape)
    return pl.BlockSpec(shape, lambda i, *_: zeros)


def sum_blocks(ids_all, g, adapters):
    shape = (adapters,) + g.shape[2:]
    return pl.pallas_call(
        sum_kernel,
        in_specs=[SMEM, VMEM],
        out_specs=VMEM,
        out_shape=pltpu.HBM(shape, BF16),
        scratch_shapes=[pltpu.VMEM(shape, F32)],
        compiler_params=vmem(16),
        cost_estimate=cost(g.size, 4 * g.size),
        name="sum_blocks",
    )(ids_all, g)


def body(tokens, weight, down, up, dy, ids, fill):
    rows_dev, width = tokens.shape
    value = dy.shape[1]
    blocks = ids.shape[0]
    slots, feats, rank = down.shape
    cols = up.shape[2]
    ys, xhs = lax.axis_size("y"), lax.axis_size("xh")
    steps = lax.axis_size(FSDP)
    adapters = slots * ys * xhs
    y_at, xh_at = lax.axis_index("y"), lax.axis_index("xh")
    z_at, xl_at, c_at = (lax.axis_index(a) for a in FSDP)
    ids_out = jnp.broadcast_to(jnp.pad(ids, (0, 128 - blocks)), (steps, 8, 128))
    ids_all = exchange(ids_out, FSDP)

    quarter = feats // ys
    mine = lax.dynamic_slice_in_dim(weight, y_at * quarter, quarter)
    rest = [shift(mine, "z", by) for by in (1, -1, 2)]

    folds = feats // rank
    up_t = jnp.swapaxes(up, 1, 2).reshape(slots, folds, cols // folds, rank)
    up_packed = jnp.swapaxes(up_t, 1, 2).reshape(slots, cols // folds, feats)
    own = jnp.concatenate([jnp.swapaxes(down, 1, 2), up_packed], axis=1)
    x_all = jnp.stack([own, shift(own, "xh", 1)])
    one, three = shift(x_all, "y", 1), shift(x_all, "y", -1)

    across = [(0, 3), (3, 0), (1, 2), (2, 1)]
    ring = jnp.stack(rest)
    ring_x = lax.ppermute(ring, X, across)

    lo = shift(gate(one, ids_all)[:, : slots // 2], "y", 1)
    hi = shift(gate(three, ids_all)[:, slots // 2 :], "y", -1)
    every = jnp.stack([x_all, one, jnp.concatenate([lo, hi], axis=1), three])

    ids_all = ids_all[:, 0, :blocks]
    want = ids_all.reshape(steps * blocks)
    owner = want // slots
    oy, ox = (y_at - owner // xhs) % ys, (xh_at - owner % xhs) % xhs
    at = (oy * xhs + ox) * slots + want % slots
    picked = every.reshape(adapters, *own.shape[1:])[at].reshape(steps, blocks, *own.shape[1:])
    low = exchange(gate(picked, ring_x), FSDP)

    w_x = lax.ppermute(gate(weight, picked), X, across)
    ring = jnp.concatenate([gate(ring, picked), ring_x])
    y_back, y_next = shift(ring, "y", 1), shift(ring, "y", -1)

    grid = 2
    per = steps // grid
    x_spec = pl.BlockSpec((rows_dev, per * feats), lambda i: (0, i))
    up_rows = cols // folds
    low_v, low_u, up_mine, grads = pl.pallas_call(
        functools.partial(low_kernel, blocks, per),
        grid=(grid,),
        in_specs=[
            SMEM,
            x_spec,
            whole(dy.shape),
            pl.BlockSpec((steps, blocks, up_rows, feats), lambda i: (0, 0, rank // up_rows, 0)),
            pl.BlockSpec((per, blocks, rank, feats), lambda i: (i, 0, 0, 0)),
        ],
        out_specs=[
            whole((rows_dev, rank)),
            whole((rows_dev, rank)),
            whole((blocks, value, rank)),
            whole(low.shape),
        ],
        out_shape=[
            pltpu.HBM((rows_dev, rank), BF16),
            pltpu.HBM((rows_dev, rank), BF16),
            pltpu.HBM((blocks, value, rank), BF16),
            pltpu.HBM(low.shape, BF16),
        ],
        scratch_shapes=[pltpu.VMEM((rows_dev, rank), F32)],
        compiler_params=vmem(24),
        cost_estimate=cost(rows_dev * rank * 4 * (width + value), 16 << 20),
        name="low",
    )(fill, *(hbm(a) for a in (tokens, dy, low, low)))
    y_lo = shift(gate(y_back, low_u)[:3], "y", 1)
    y_hi = shift(gate(y_next, low_u)[3:], "y", -1)
    back = exchange(gate(grads, y_back, y_next), FSDP)

    w_own = [weight, w_x, ring, y_back, y_next, y_lo, y_hi]
    w_all = w_own + [shift(gate(w, low_u), "c", 1) for w in w_own]
    order = [
        (z_at + dz) % 4 * 4 + (xl_at + dx) % 2 * 2 + (c_at + dc) % 2
        for dc in (0, 1)
        for dx, dz in ((0, 0), (1, 0), (0, 3), (0, 1), (0, 2), (1, 3), (1, 1), (1, 2))
    ] + [(y_at + dy) % ys * quarter for dy in (0, 3, 1, 2)]

    values, input_gradient = pl.pallas_call(
        functools.partial(base_kernel, blocks, quarter),
        grid_spec=pltpu.PrefetchScalarGridSpec(
            num_scalar_prefetch=1,
            grid=(steps,),
            in_specs=[
                pl.BlockSpec((rows_dev, feats), lambda i, f: (0, f[i])),
                whole(dy.shape),
                whole(low_u.shape),
                whole(low_v.shape),
                whole(up_mine.shape),
                pl.BlockSpec((1, blocks, rank, feats), lambda i, f: (f[i], 0, 0, 0)),
            ]
            + [pl.BlockSpec(memory_space=pltpu.HBM)] * len(w_all),
            out_specs=[
                whole((rows_dev, value)),
                pl.BlockSpec((rows_dev, feats), lambda i, f: (0, f[i])),
            ],
            scratch_shapes=[
                pltpu.VMEM((rows_dev, value), F32),
                pltpu.VMEM((2, feats, value), BF16),
                pltpu.SemaphoreType.DMA((2,)),
            ],
        ),
        out_shape=[pltpu.HBM((rows_dev, value), BF16), pltpu.HBM((rows_dev, width), BF16)],
        compiler_params=vmem(28),
        cost_estimate=cost(4 * rows_dev * width * value, 36 << 20),
        name="base",
    )(
        jnp.stack(order),
        *(hbm(a) for a in (tokens, dy, low_u, low_v, up_mine, low)),
        *(hbm(a) for a in w_all),
    )

    part = exchange(sum_blocks(ids_all, back, adapters), DP)
    part = gate(part, values).reshape(ys * xhs, slots, *own.shape[1:])
    total = SCALE * part.astype(F32).sum(0)
    grad_down = total[:, :rank]
    grad_up = total[:, rank:].reshape(slots, up_rows, folds, rank)
    grad_up = jnp.transpose(grad_up, (0, 3, 2, 1)).reshape(slots, rank, cols)
    return values, input_gradient, jnp.swapaxes(grad_down, 1, 2), grad_up


def solution(mesh):
    fine = Mesh(mesh.devices.reshape(4, 2, 4, 2, 2), DP + FSDP)
    every = DP + FSDP
    placed = (
        P(every, None),
        P(FSDP, None),
        P(DP, FSDP, None),
        P(DP, None, FSDP),
        P(every, None),
        P(every),
        P(every),
    )
    return jax.shard_map(
        body,
        mesh=fine,
        in_specs=placed,
        out_specs=(P(every, None), P(every, None), P(DP, FSDP, None), P(DP, None, FSDP)),
        check_vma=False,
    )
```

```python
import functools

import jax
import jax.numpy as jnp
from jax import lax
from jax.experimental import pallas as pl
from jax.experimental.pallas import tpu as pltpu
from jax.sharding import Mesh
from jax.sharding import PartitionSpec as P

DP = ("y", "xh")
FSDP = ("z", "xl", "c")
X = ("xh", "xl")
SCALE = 0.5
F32 = jnp.float32
BF16 = jnp.bfloat16


def nt(a, b):
    return lax.dot_general(a, b, (((1,), (1,)), ((), ())), preferred_element_type=F32)


def tn(a, b):
    return lax.dot_general(a, b, (((0,), (0,)), ((), ())), preferred_element_type=F32)


def nn(a, b):
    return jnp.dot(a, b, preferred_element_type=F32)


def shift(x, axis, by):
    n = lax.axis_size(axis)
    return lax.ppermute(x, axis, [(i, (i + by) % n) for i in range(n)])


def gate(x, *needed):
    return lax.optimization_barrier((x, *needed))[0]


def exchange(x, axis):
    return lax.all_to_all(x, axis, split_axis=0, concat_axis=0, tiled=True)


def hbm(x):
    return pltpu.with_memory_space_constraint(x, pltpu.HBM)


def live_rows(fill_ref, b, rows):
    return (lax.broadcasted_iota(jnp.int32, (rows, 1), 0) < fill_ref[b]).astype(F32)


def pack(a, k):
    n = a.shape[0] // k
    return jnp.concatenate([a[i * n : (i + 1) * n] for i in range(k)], axis=1)


def unpack(a, k):
    r = a.shape[1] // k
    return jnp.concatenate([a[:, i * r : (i + 1) * r] for i in range(k)], axis=0)


def low_kernel(blocks, per, fill_ref, x_ref, dy_ref, packed_ref, down_ref, v_ref, u_ref, up_ref, g_ref, acc_ref):
    rows = dy_ref.shape[0] // blocks
    rank, feats = down_ref.shape[2:]
    steps = g_ref.shape[0]
    cols = dy_ref.shape[1] // steps
    step = pl.program_id(0)

    @pl.when(step == 0)
    def _():
        acc_ref[...] = jnp.zeros_like(acc_ref)
        for b in range(blocks):
            at = pl.ds(b * rows, rows)
            for f in range(steps):
                up_ref[b, pl.ds(f * cols, cols), :] = unpack(packed_ref[f, b], cols // packed_ref.shape[2])
            v = nn(dy_ref[at, :], up_ref[b]) * live_rows(fill_ref, b, rows)
            v_ref[at, :] = v.astype(BF16)

    for b in range(blocks):
        at = pl.ds(b * rows, rows)
        v = v_ref[at, :]
        total = acc_ref[at, :]
        for j in range(per):
            x = x_ref[at, pl.ds(j * feats, feats)]
            total += nt(x, down_ref[j, b])
            g_ref[step * per + j, b, :rank, :] = tn(v, x).astype(BF16)
        acc_ref[at, :] = total

    @pl.when(step == pl.num_programs(0) - 1)
    def _():
        for b in range(blocks):
            at = pl.ds(b * rows, rows)
            u = (acc_ref[at, :] * live_rows(fill_ref, b, rows)).astype(BF16)
            u_ref[at, :] = u
            g = tn(dy_ref[at, :], u).astype(BF16)
            for f in range(steps):
                g_ref[f, b, rank:, :] = pack(g[f * cols : (f + 1) * cols], feats // rank)


def base_kernel(blocks, quarter, f_ref, x_ref, dy_ref, u_ref, v_ref, up_ref, down_ref, *refs):
    w_refs, (y_ref, dx_ref, acc_ref, w_buf, sem) = refs[:-5], refs[-5:]
    rows = dy_ref.shape[0] // blocks
    step, steps = pl.program_id(0), pl.num_programs(0)
    feats = w_buf.shape[1]
    per = steps // 2

    def fetch(i):
        slot, m = i % 2, i % per

        def start(src, k):
            to = w_buf.at[slot, pl.ds(pl.multiple_of(f_ref[steps + k], quarter), quarter)]
            pltpu.make_async_copy(src, to, sem.at[slot]).start()

        for core in range(2):
            own, x, ring, back, ahead, lo, hi = w_refs[7 * core : 7 * core + 7]
            for k, w_ref in enumerate((own, x)):

                @pl.when(i == core * per + k)
                def _():
                    pltpu.make_async_copy(w_ref, w_buf.at[slot], sem.at[slot]).start()

            @pl.when((i // per == core) & (m >= 2))
            def _():
                for k, w_ref in enumerate((ring, back, ahead)):
                    start(w_ref.at[m - 2], k)

            @pl.when((i // per == core) & (m >= 2) & (m < 5))
            def _():
                start(lo.at[m - 2], 3)

            @pl.when((i // per == core) & (m >= 5))
            def _():
                start(hi.at[m - 5], 3)

    @pl.when(step == 0)
    def _():
        acc_ref[...] = jnp.zeros_like(acc_ref)
        fetch(step)

    @pl.when(step + 1 < steps)
    def _():
        fetch(step + 1)

    slot = step % 2
    pltpu.make_async_copy(w_refs[0], w_buf.at[slot], sem.at[slot]).wait()
    w = w_buf[slot]
    acc_ref[...] += nn(x_ref[...], w)
    wide = nt(dy_ref[...], w)
    for b in range(blocks):
        at = pl.ds(b * rows, rows)
        pulled = nn(v_ref[at, :], down_ref[0, b]).astype(BF16).astype(F32)
        dx_ref[at, :] = (wide[b * rows : (b + 1) * rows, :] + SCALE * pulled).astype(BF16)

    @pl.when(step == steps - 1)
    def _():
        for b in range(blocks):
            at = pl.ds(b * rows, rows)
            lifted = nt(u_ref[at, :], up_ref[b]).astype(BF16).astype(F32)
            y_ref[at, :] = (acc_ref[at, :] + SCALE * lifted).astype(BF16)


def sum_kernel(ids_ref, g_ref, o_ref, acc_ref):
    members, blocks = g_ref.shape[:2]
    acc_ref[...] = jnp.zeros_like(acc_ref)

    @pl.loop(0, members)
    def _(m):
        for b in range(blocks):
            acc_ref[ids_ref[m, b]] += g_ref[m, b].astype(F32)

    o_ref[...] = acc_ref[...].astype(BF16)


def vmem(mib):
    return pltpu.CompilerParams(vmem_limit_bytes=mib * 1024 * 1024)


VMEM = pl.BlockSpec(memory_space=pltpu.VMEM)
SMEM = pl.BlockSpec(memory_space=pltpu.SMEM)


def cost(flops, size):
    return pl.CostEstimate(flops=flops, bytes_accessed=size, transcendentals=0)


def whole(shape):
    zeros = (0,) * len(shape)
    return pl.BlockSpec(shape, lambda i, *_: zeros)


def sum_blocks(ids_all, g, adapters):
    shape = (adapters,) + g.shape[2:]
    return pl.pallas_call(
        sum_kernel,
        in_specs=[SMEM, VMEM],
        out_specs=VMEM,
        out_shape=pltpu.HBM(shape, BF16),
        scratch_shapes=[pltpu.VMEM(shape, F32)],
        compiler_params=vmem(16),
        cost_estimate=cost(g.size, 4 * g.size),
        name="sum_blocks",
    )(ids_all, g)


def body(tokens, weight, down, up, dy, ids, fill):
    rows_dev, width = tokens.shape
    value = dy.shape[1]
    blocks = ids.shape[0]
    slots, feats, rank = down.shape
    cols = up.shape[2]
    ys, xhs = lax.axis_size("y"), lax.axis_size("xh")
    steps = lax.axis_size(FSDP)
    adapters = slots * ys * xhs
    y_at, xh_at = lax.axis_index("y"), lax.axis_index("xh")
    z_at, xl_at, c_at = (lax.axis_index(a) for a in FSDP)
    ids_out = jnp.broadcast_to(jnp.pad(ids, (0, 128 - blocks)), (steps, 8, 128))
    ids_all = exchange(ids_out, FSDP)

    quarter = feats // ys
    mine = lax.dynamic_slice_in_dim(weight, y_at * quarter, quarter)
    rest = [shift(mine, "z", by) for by in (1, -1, 2)]

    folds = feats // rank
    up_t = jnp.swapaxes(up, 1, 2).reshape(slots, folds, cols // folds, rank)
    up_packed = jnp.swapaxes(up_t, 1, 2).reshape(slots, cols // folds, feats)
    own = jnp.concatenate([jnp.swapaxes(down, 1, 2), up_packed], axis=1)
    x_all = jnp.stack([own, shift(own, "xh", 1)])
    one, three = shift(x_all, "y", 1), shift(x_all, "y", -1)

    across = [(0, 3), (3, 0), (1, 2), (2, 1)]
    ring = jnp.stack(rest)
    ring_x = lax.ppermute(ring, X, across)

    lo = shift(gate(one, ids_all)[:, : slots // 2], "y", 1)
    hi = shift(gate(three, ids_all)[:, slots // 2 :], "y", -1)
    every = jnp.stack([x_all, one, jnp.concatenate([lo, hi], axis=1), three])

    ids_all = ids_all[:, 0, :blocks]
    want = ids_all.reshape(steps * blocks)
    owner = want // slots
    oy, ox = (y_at - owner // xhs) % ys, (xh_at - owner % xhs) % xhs
    at = (oy * xhs + ox) * slots + want % slots
    picked = every.reshape(adapters, *own.shape[1:])[at].reshape(steps, blocks, *own.shape[1:])
    low = exchange(gate(picked, ring_x), FSDP)

    w_x = lax.ppermute(gate(weight, picked), X, across)
    ring = jnp.concatenate([gate(ring, picked), ring_x])
    y_back, y_next = shift(ring, "y", 1), shift(ring, "y", -1)

    grid = 2
    per = steps // grid
    x_spec = pl.BlockSpec((rows_dev, per * feats), lambda i: (0, i))
    up_rows = cols // folds
    low_v, low_u, up_mine, grads = pl.pallas_call(
        functools.partial(low_kernel, blocks, per),
        grid=(grid,),
        in_specs=[
            SMEM,
            x_spec,
            whole(dy.shape),
            pl.BlockSpec((steps, blocks, up_rows, feats), lambda i: (0, 0, rank // up_rows, 0)),
            pl.BlockSpec((per, blocks, rank, feats), lambda i: (i, 0, 0, 0)),
        ],
        out_specs=[
            whole((rows_dev, rank)),
            whole((rows_dev, rank)),
            whole((blocks, value, rank)),
            whole(low.shape),
        ],
        out_shape=[
            pltpu.HBM((rows_dev, rank), BF16),
            pltpu.HBM((rows_dev, rank), BF16),
            pltpu.HBM((blocks, value, rank), BF16),
            pltpu.HBM(low.shape, BF16),
        ],
        scratch_shapes=[pltpu.VMEM((rows_dev, rank), F32)],
        compiler_params=vmem(24),
        cost_estimate=cost(rows_dev * rank * 4 * (width + value), 16 << 20),
        name="low",
    )(fill, *(hbm(a) for a in (tokens, dy, low, low)))
    y_lo = shift(gate(y_back, low_u)[:3], "y", 1)
    y_hi = shift(gate(y_next, low_u)[3:], "y", -1)
    back = exchange(gate(grads, y_back, y_next), FSDP)

    w_own = [weight, w_x, ring, y_back, y_next, y_lo, y_hi]
    w_all = w_own + [shift(gate(w, low_u), "c", 1) for w in w_own]
    back = gate(back, *w_all)
    order = [
        (z_at + dz) % 4 * 4 + (xl_at + dx) % 2 * 2 + (c_at + dc) % 2
        for dc in (0, 1)
        for dx, dz in ((0, 0), (1, 0), (0, 3), (0, 1), (0, 2), (1, 3), (1, 1), (1, 2))
    ] + [(y_at + dy) % ys * quarter for dy in (0, 3, 1, 2)]

    values, input_gradient = pl.pallas_call(
        functools.partial(base_kernel, blocks, quarter),
        grid_spec=pltpu.PrefetchScalarGridSpec(
            num_scalar_prefetch=1,
            grid=(steps,),
            in_specs=[
                pl.BlockSpec((rows_dev, feats), lambda i, f: (0, f[i])),
                whole(dy.shape),
                whole(low_u.shape),
                whole(low_v.shape),
                whole(up_mine.shape),
                pl.BlockSpec((1, blocks, rank, feats), lambda i, f: (f[i], 0, 0, 0)),
            ]
            + [pl.BlockSpec(memory_space=pltpu.HBM)] * len(w_all),
            out_specs=[
                whole((rows_dev, value)),
                pl.BlockSpec((rows_dev, feats), lambda i, f: (0, f[i])),
            ],
            scratch_shapes=[
                pltpu.VMEM((rows_dev, value), F32),
                pltpu.VMEM((2, feats, value), BF16),
                pltpu.SemaphoreType.DMA((2,)),
            ],
        ),
        out_shape=[pltpu.HBM((rows_dev, value), BF16), pltpu.HBM((rows_dev, width), BF16)],
        compiler_params=vmem(28),
        cost_estimate=cost(4 * rows_dev * width * value, 36 << 20),
        name="base",
    )(
        jnp.stack(order),
        *(hbm(a) for a in (tokens, dy, low_u, low_v, up_mine, low)),
        *(hbm(a) for a in w_all),
    )

    part = exchange(sum_blocks(ids_all, back, adapters), DP)
    part = gate(part, values).reshape(ys * xhs, slots, *own.shape[1:])
    total = SCALE * part.astype(F32).sum(0)
    grad_down = total[:, :rank]
    grad_up = total[:, rank:].reshape(slots, up_rows, folds, rank)
    grad_up = jnp.transpose(grad_up, (0, 3, 2, 1)).reshape(slots, rank, cols)
    return values, input_gradient, jnp.swapaxes(grad_down, 1, 2), grad_up


def solution(mesh):
    fine = Mesh(mesh.devices.reshape(4, 2, 4, 2, 2), DP + FSDP)
    every = DP + FSDP
    placed = (
        P(every, None),
        P(FSDP, None),
        P(DP, FSDP, None),
        P(DP, None, FSDP),
        P(every, None),
        P(every),
        P(every),
    )
    return jax.shard_map(
        body,
        mesh=fine,
        in_specs=placed,
        out_specs=(P(every, None), P(every, None), P(DP, FSDP, None), P(DP, None, FSDP)),
        check_vma=False,
    )
```

```python
import functools

import jax
import jax.numpy as jnp
from jax import lax
from jax.experimental import pallas as pl
from jax.experimental.pallas import tpu as pltpu
from jax.sharding import Mesh
from jax.sharding import PartitionSpec as P

DP = ("y", "xh")
FSDP = ("z", "xl", "c")
X = ("xh", "xl")
SCALE = 0.5
F32 = jnp.float32
BF16 = jnp.bfloat16


def nt(a, b):
    return lax.dot_general(a, b, (((1,), (1,)), ((), ())), preferred_element_type=F32)


def tn(a, b):
    return lax.dot_general(a, b, (((0,), (0,)), ((), ())), preferred_element_type=F32)


def nn(a, b):
    return jnp.dot(a, b, preferred_element_type=F32)


def shift(x, axis, by):
    n = lax.axis_size(axis)
    return lax.ppermute(x, axis, [(i, (i + by) % n) for i in range(n)])


def gate(x, *needed):
    return lax.optimization_barrier((x, *needed))[0]


def exchange(x, axis):
    return lax.all_to_all(x, axis, split_axis=0, concat_axis=0, tiled=True)


def hbm(x):
    return pltpu.with_memory_space_constraint(x, pltpu.HBM)


def live_rows(fill_ref, b, rows):
    return (lax.broadcasted_iota(jnp.int32, (rows, 1), 0) < fill_ref[b]).astype(F32)


def pack(a, k):
    n = a.shape[0] // k
    return jnp.concatenate([a[i * n : (i + 1) * n] for i in range(k)], axis=1)


def unpack(a, k):
    r = a.shape[1] // k
    return jnp.concatenate([a[:, i * r : (i + 1) * r] for i in range(k)], axis=0)


def low_kernel(blocks, per, fill_ref, x_ref, dy_ref, packed_ref, down_ref, v_ref, u_ref, up_ref, g_ref, acc_ref):
    rows = dy_ref.shape[0] // blocks
    rank, feats = down_ref.shape[2:]
    steps = g_ref.shape[0]
    cols = dy_ref.shape[1] // steps
    step = pl.program_id(0)

    @pl.when(step == 0)
    def _():
        acc_ref[...] = jnp.zeros_like(acc_ref)
        for b in range(blocks):
            at = pl.ds(b * rows, rows)
            for f in range(steps):
                up_ref[b, pl.ds(f * cols, cols), :] = unpack(packed_ref[f, b], cols // packed_ref.shape[2])
            v = nn(dy_ref[at, :], up_ref[b]) * live_rows(fill_ref, b, rows)
            v_ref[at, :] = v.astype(BF16)

    for b in range(blocks):
        at = pl.ds(b * rows, rows)
        v = v_ref[at, :]
        total = acc_ref[at, :]
        for j in range(per):
            x = x_ref[at, pl.ds(j * feats, feats)]
            total += nt(x, down_ref[j, b])
            g_ref[step * per + j, b, :rank, :] = tn(v, x).astype(BF16)
        acc_ref[at, :] = total

    @pl.when(step == pl.num_programs(0) - 1)
    def _():
        for b in range(blocks):
            at = pl.ds(b * rows, rows)
            u = (acc_ref[at, :] * live_rows(fill_ref, b, rows)).astype(BF16)
            u_ref[at, :] = u
            g = tn(dy_ref[at, :], u).astype(BF16)
            for f in range(steps):
                g_ref[f, b, rank:, :] = pack(g[f * cols : (f + 1) * cols], feats // rank)


def base_kernel(blocks, quarter, f_ref, x_ref, dy_ref, u_ref, v_ref, up_ref, down_ref, *refs):
    w_refs, (y_ref, dx_ref, acc_ref, w_buf, sem) = refs[:-5], refs[-5:]
    rows = dy_ref.shape[0] // blocks
    step, steps = pl.program_id(0), pl.num_programs(0)
    feats = w_buf.shape[1]
    per = steps // 2

    def fetch(i):
        slot, m = i % 2, i % per

        def start(src, k):
            to = w_buf.at[slot, pl.ds(pl.multiple_of(f_ref[steps + k], quarter), quarter)]
            pltpu.make_async_copy(src, to, sem.at[slot]).start()

        for core in range(2):
            own, x, ring, back, ahead, lo, hi = w_refs[7 * core : 7 * core + 7]
            for k, w_ref in enumerate((own, x)):

                @pl.when(i == core * per + k)
                def _():
                    pltpu.make_async_copy(w_ref, w_buf.at[slot], sem.at[slot]).start()

            @pl.when((i // per == core) & (m >= 2))
            def _():
                for k, w_ref in enumerate((ring, back, ahead)):
                    start(w_ref.at[m - 2], k)

            @pl.when((i // per == core) & (m >= 2) & (m < 5))
            def _():
                start(lo.at[m - 2], 3)

            @pl.when((i // per == core) & (m >= 5))
            def _():
                start(hi.at[m - 5], 3)

    @pl.when(step == 0)
    def _():
        acc_ref[...] = jnp.zeros_like(acc_ref)
        fetch(step)

    @pl.when(step + 1 < steps)
    def _():
        fetch(step + 1)

    slot = step % 2
    pltpu.make_async_copy(w_refs[0], w_buf.at[slot], sem.at[slot]).wait()
    w = w_buf[slot]
    acc_ref[...] += nn(x_ref[...], w)
    wide = nt(dy_ref[...], w)
    for b in range(blocks):
        at = pl.ds(b * rows, rows)
        pulled = nn(v_ref[at, :], down_ref[0, b]).astype(BF16).astype(F32)
        dx_ref[at, :] = (wide[b * rows : (b + 1) * rows, :] + SCALE * pulled).astype(BF16)

    @pl.when(step == steps - 1)
    def _():
        for b in range(blocks):
            at = pl.ds(b * rows, rows)
            lifted = nt(u_ref[at, :], up_ref[b]).astype(BF16).astype(F32)
            y_ref[at, :] = (acc_ref[at, :] + SCALE * lifted).astype(BF16)


def sum_kernel(ids_ref, g_ref, o_ref, acc_ref):
    members, blocks = g_ref.shape[:2]
    acc_ref[...] = jnp.zeros_like(acc_ref)

    @pl.loop(0, members)
    def _(m):
        for b in range(blocks):
            acc_ref[ids_ref[m, b]] += g_ref[m, b].astype(F32)

    o_ref[...] = acc_ref[...].astype(BF16)


def vmem(mib):
    return pltpu.CompilerParams(vmem_limit_bytes=mib * 1024 * 1024)


VMEM = pl.BlockSpec(memory_space=pltpu.VMEM)
SMEM = pl.BlockSpec(memory_space=pltpu.SMEM)


def cost(flops, size):
    return pl.CostEstimate(flops=flops, bytes_accessed=size, transcendentals=0)


def whole(shape):
    zeros = (0,) * len(shape)
    return pl.BlockSpec(shape, lambda i, *_: zeros)


def sum_blocks(ids_all, g, adapters):
    shape = (adapters,) + g.shape[2:]
    return pl.pallas_call(
        sum_kernel,
        in_specs=[SMEM, VMEM],
        out_specs=VMEM,
        out_shape=pltpu.HBM(shape, BF16),
        scratch_shapes=[pltpu.VMEM(shape, F32)],
        compiler_params=vmem(16),
        cost_estimate=cost(g.size, 4 * g.size),
        name="sum_blocks",
    )(ids_all, g)


def body(tokens, weight, down, up, dy, ids, fill):
    rows_dev, width = tokens.shape
    value = dy.shape[1]
    blocks = ids.shape[0]
    slots, feats, rank = down.shape
    cols = up.shape[2]
    ys, xhs = lax.axis_size("y"), lax.axis_size("xh")
    steps = lax.axis_size(FSDP)
    adapters = slots * ys * xhs
    y_at, xh_at = lax.axis_index("y"), lax.axis_index("xh")
    z_at, xl_at, c_at = (lax.axis_index(a) for a in FSDP)
    ids_out = jnp.broadcast_to(jnp.pad(ids, (0, 128 - blocks)), (steps, 8, 128))
    ids_all = exchange(ids_out, FSDP)

    quarter = feats // ys
    mine = lax.dynamic_slice_in_dim(weight, y_at * quarter, quarter)
    rest = [shift(mine, "z", by) for by in (1, -1, 2)]

    folds = feats // rank
    up_t = jnp.swapaxes(up, 1, 2).reshape(slots, folds, cols // folds, rank)
    up_packed = jnp.swapaxes(up_t, 1, 2).reshape(slots, cols // folds, feats)
    own = jnp.concatenate([jnp.swapaxes(down, 1, 2), up_packed], axis=1)
    x_all = jnp.stack([own, shift(own, "xh", 1)])
    one, three = shift(x_all, "y", 1), shift(x_all, "y", -1)

    across = [(0, 3), (3, 0), (1, 2), (2, 1)]
    ring = jnp.stack(rest)
    early = quarter * 7 // 8
    x_early = lax.ppermute(jnp.stack([r[:early] for r in rest]), X, across)

    lo = shift(gate(one, ids_all)[:, : slots // 2], "y", 1)
    hi = shift(gate(three, ids_all)[:, slots // 2 :], "y", -1)
    every = jnp.stack([x_all, one, jnp.concatenate([lo, hi], axis=1), three])

    ids_all = ids_all[:, 0, :blocks]
    want = ids_all.reshape(steps * blocks)
    owner = want // slots
    oy, ox = (y_at - owner // xhs) % ys, (xh_at - owner % xhs) % xhs
    at = (oy * xhs + ox) * slots + want % slots
    picked = every.reshape(adapters, *own.shape[1:])[at].reshape(steps, blocks, *own.shape[1:])
    low = exchange(gate(picked, x_early), FSDP)

    w_x = lax.ppermute(gate(weight, picked), X, across)
    x_late = lax.ppermute(gate(ring, picked)[:, early:], X, across)
    ring = jnp.concatenate([gate(ring, picked), jnp.concatenate([x_early, x_late], axis=1)])
    y_back, y_next = shift(ring, "y", 1), shift(ring, "y", -1)

    grid = 2
    per = steps // grid
    x_spec = pl.BlockSpec((rows_dev, per * feats), lambda i: (0, i))
    up_rows = cols // folds
    low_v, low_u, up_mine, grads = pl.pallas_call(
        functools.partial(low_kernel, blocks, per),
        grid=(grid,),
        in_specs=[
            SMEM,
            x_spec,
            whole(dy.shape),
            pl.BlockSpec((steps, blocks, up_rows, feats), lambda i: (0, 0, rank // up_rows, 0)),
            pl.BlockSpec((per, blocks, rank, feats), lambda i: (i, 0, 0, 0)),
        ],
        out_specs=[
            whole((rows_dev, rank)),
            whole((rows_dev, rank)),
            whole((blocks, value, rank)),
            whole(low.shape),
        ],
        out_shape=[
            pltpu.HBM((rows_dev, rank), BF16),
            pltpu.HBM((rows_dev, rank), BF16),
            pltpu.HBM((blocks, value, rank), BF16),
            pltpu.HBM(low.shape, BF16),
        ],
        scratch_shapes=[pltpu.VMEM((rows_dev, rank), F32)],
        compiler_params=vmem(24),
        cost_estimate=cost(rows_dev * rank * 4 * (width + value), 16 << 20),
        name="low",
    )(fill, *(hbm(a) for a in (tokens, dy, low, low)))
    y_lo = shift(gate(y_back, low_u)[:3], "y", 1)
    y_hi = shift(gate(y_next, low_u)[3:], "y", -1)
    back = exchange(gate(grads, y_back, y_next), FSDP)

    w_own = [weight, w_x, ring, y_back, y_next, y_lo, y_hi]
    w_all = w_own + [shift(gate(w, low_u), "c", 1) for w in w_own]
    order = [
        (z_at + dz) % 4 * 4 + (xl_at + dx) % 2 * 2 + (c_at + dc) % 2
        for dc in (0, 1)
        for dx, dz in ((0, 0), (1, 0), (0, 3), (0, 1), (0, 2), (1, 3), (1, 1), (1, 2))
    ] + [(y_at + dy) % ys * quarter for dy in (0, 3, 1, 2)]

    values, input_gradient = pl.pallas_call(
        functools.partial(base_kernel, blocks, quarter),
        grid_spec=pltpu.PrefetchScalarGridSpec(
            num_scalar_prefetch=1,
            grid=(steps,),
            in_specs=[
                pl.BlockSpec((rows_dev, feats), lambda i, f: (0, f[i])),
                whole(dy.shape),
                whole(low_u.shape),
                whole(low_v.shape),
                whole(up_mine.shape),
                pl.BlockSpec((1, blocks, rank, feats), lambda i, f: (f[i], 0, 0, 0)),
            ]
            + [pl.BlockSpec(memory_space=pltpu.HBM)] * len(w_all),
            out_specs=[
                whole((rows_dev, value)),
                pl.BlockSpec((rows_dev, feats), lambda i, f: (0, f[i])),
            ],
            scratch_shapes=[
                pltpu.VMEM((rows_dev, value), F32),
                pltpu.VMEM((2, feats, value), BF16),
                pltpu.SemaphoreType.DMA((2,)),
            ],
        ),
        out_shape=[pltpu.HBM((rows_dev, value), BF16), pltpu.HBM((rows_dev, width), BF16)],
        compiler_params=vmem(28),
        cost_estimate=cost(4 * rows_dev * width * value, 36 << 20),
        name="base",
    )(
        jnp.stack(order),
        *(hbm(a) for a in (tokens, dy, low_u, low_v, up_mine, low)),
        *(hbm(a) for a in w_all),
    )

    part = exchange(sum_blocks(ids_all, back, adapters), DP)
    part = gate(part, values).reshape(ys * xhs, slots, *own.shape[1:])
    total = SCALE * part.astype(F32).sum(0)
    grad_down = total[:, :rank]
    grad_up = total[:, rank:].reshape(slots, up_rows, folds, rank)
    grad_up = jnp.transpose(grad_up, (0, 3, 2, 1)).reshape(slots, rank, cols)
    return values, input_gradient, jnp.swapaxes(grad_down, 1, 2), grad_up


def solution(mesh):
    fine = Mesh(mesh.devices.reshape(4, 2, 4, 2, 2), DP + FSDP)
    every = DP + FSDP
    placed = (
        P(every, None),
        P(FSDP, None),
        P(DP, FSDP, None),
        P(DP, None, FSDP),
        P(every, None),
        P(every),
        P(every),
    )
    return jax.shard_map(
        body,
        mesh=fine,
        in_specs=placed,
        out_specs=(P(every, None), P(every, None), P(DP, FSDP, None), P(DP, None, FSDP)),
        check_vma=False,
    )
```
